256 devices in a mesh: blk: 64 (over y, z, core), band: 4 (over x).
Axes of the slice: x: 4, y: 4, z: 8, core: 2. Of those that a mesh axis runs over, the one named last changes fastest.
Arguments:
- sky_map: float32 [2, 512, 16384], P(None, 'blk'), may hold values from -6 to 6
- cycle_counts: int32 [512], P('blk'), may hold values from 8192 to 16384, as said below
- legendre: bfloat16 [512, 256, 4096], P(None, ('blk', 'band')), may hold values from -0.25 to 0.25
- signal_power: float32 [8192], replicated, may hold values from 0.1 to 10
- noise_power: float32 [8192], replicated, may hold values from 0.1 to 10
Outputs:
- filtered_map: float32 [2, 512, 16384], P(None, 'blk', 'band')
The draws below stay inside these ranges and needn't reach their ends.
Inputs may be any that keep to these rules, and one draw needn't show every extreme that they name: `cycle_counts`: every cycle pair has between 8192 and 16384 pixels, and some cycle pair has exactly 16384.
All inputs are finite; a program needn't handle non-finite values.
Results may differ from the reference program's by a relative error of at most 0.0061.
Values may be sent and summed in bfloat16 or wider, within the bound.
A program may use at most 128 MiB of HBM per device.

```python
import math
import jax
import jax.numpy as jnp
from jax import lax

NPHI = 16384
NL = 4096
LMAX = 8191
M_FIRST = 2048
M_DEV = 1
RH_TOT = 512
M = 256
N_BLK = 64
N_BAND = 4


def draw_cycle_counts(key, part):
    first, second = jax.random.split(key)
    counts = jax.random.randint(first, (RH_TOT,), NPHI // 2, NPHI + 1)
    spot = jax.random.randint(second, (), 0, RH_TOT)
    return jnp.where(jnp.arange(RH_TOT) == spot, NPHI, counts).astype(jnp.int32)


def levels(own_key, extent, cuts, low, top_value):
    def one(dim, parts):
        steps = jax.random.uniform(jax.random.fold_in(jax.random.fold_in(own_key, 6), dim), (parts,), jnp.float32, low / len(cuts), top_value / len(cuts))
        return jnp.repeat(jnp.exp(steps), extent[dim] // parts).reshape((-1,) + (1,) * (len(extent) - dim - 1))

    factor_of = one(*cuts[0])
    for cut in cuts[1:]:
        factor_of = factor_of * one(*cut)
    return factor_of


def normal_values(key, extent, deviation, limit, cuts=(), kind=jnp.bfloat16):
    array = deviation * jax.random.normal(key, extent, jnp.float32)
    if cuts:
        array = array * levels(key, extent, cuts, -0.22, 0.18)
    return jnp.clip(array, -limit, limit).astype(kind)


def setup_inputs(seed: int = 0) -> dict:
    seeds = jax.random.split(jax.random.key(seed), 6)
    sky_map = normal_values(seeds[0], (2, RH_TOT, NPHI), 1.0, 6.0, ((1, 64),), jnp.float32)
    cycle_counts = draw_cycle_counts(jax.random.fold_in(seeds[5], 71), 0)
    legendre = normal_values(seeds[2], (RH_TOT, M, NL), RH_TOT ** -0.5, 0.25, ((1, 256),))
    signal_power = jnp.clip(jnp.exp(jax.random.uniform(seeds[3], (LMAX + 1,), jnp.float32, math.log(0.1), math.log(10.0))), 0.1, 10.0)
    noise_power = jnp.clip(jnp.exp(jax.random.uniform(seeds[4], (LMAX + 1,), jnp.float32, math.log(0.1), math.log(10.0))), 0.1, 10.0)
    return {"sky_map": sky_map, "cycle_counts": cycle_counts, "legendre": legendre, "signal_power": signal_power, "noise_power": noise_power}


def angle_tables(frequencies, counts, odd_steps):
    period = 2 * counts
    residue = frequencies[None, :, None] * odd_steps[None, None, :] % period[:, None, None]
    angles = math.pi * residue.astype(jnp.float32) / counts.astype(jnp.float32)[:, None, None]
    return (jnp.cos(angles), jnp.sin(angles))

def make_tables(counts, inner_freq, outer_freq, odd_steps):
    cos_in, sin_in = angle_tables(inner_freq, counts, odd_steps)
    cos_out, sin_out = angle_tables(outer_freq, counts, odd_steps)
    return (cos_in, sin_in, cos_out.astype(jnp.bfloat16), sin_out.astype(jnp.bfloat16))

def batched(form, left, right):
    return jnp.einsum(form, left.astype(jnp.float32), right.astype(jnp.float32), precision=lax.Precision.HIGHEST)

def analyse(pixels, counts, tables_now, odd_steps):
    cos_in, sin_in, cos_out, sin_out = tables_now
    live_mask = (odd_steps[None, :] < 2 * counts[:, None]).astype(jnp.float32)
    weights = live_mask / jnp.sqrt(counts.astype(jnp.float32))[:, None]
    weighted = pixels * weights[None]
    part_re = (weighted[:, :, None, :] * cos_in[None]).astype(jnp.bfloat16)
    part_im = (-(weighted[:, :, None, :] * sin_in[None])).astype(jnp.bfloat16)
    real_part = batched('hbkj,bpj->hbpk', part_re, cos_out) + batched('hbkj,bpj->hbpk', part_im, sin_out)
    imag_part = batched('hbkj,bpj->hbpk', part_im, cos_out) - batched('hbkj,bpj->hbpk', part_re, sin_out)
    return (real_part, imag_part)

def synthesise(mode_re, mode_im, counts, tables_now, odd_steps, norm_factor):
    cos_in, sin_in, cos_out, sin_out = tables_now
    upper_sum = batched('hbpk,bpj->hbkj', mode_re, cos_out) - batched('hbpk,bpj->hbkj', mode_im, sin_out)
    lower_sum = batched('hbpk,bpj->hbkj', mode_re, sin_out) + batched('hbpk,bpj->hbkj', mode_im, cos_out)
    summed = lax.optimization_barrier(jnp.sum(cos_in[None] * upper_sum - sin_in[None] * lower_sum, axis=2))
    live_mask = (odd_steps[None, :] < 2 * counts[:, None]).astype(jnp.float32)
    return summed * (live_mask * norm_factor)[None]

def reference(sky_map, cycle_counts, legendre, signal_power, noise_power):
    cycle_total = sky_map.shape[1]
    slot_count = sky_map.shape[2]
    order_total = legendre.shape[1]
    degree_count = legendre.shape[2]
    c_count = N_BAND * M_DEV
    q_count = 8
    p_count = N_BLK // 8
    inner_freq = (M_FIRST + jnp.arange(c_count)[None, :] + c_count * jnp.arange(q_count)[:, None]).reshape(-1).astype(jnp.int32)
    outer_freq = (c_count * q_count * jnp.arange(p_count)).astype(jnp.int32)
    odd_steps = (2 * jnp.arange(slot_count) + 1).astype(jnp.int32)
    block_rows = 8
    blocks = cycle_total // block_rows
    map_blocks = sky_map.reshape(2, blocks, block_rows, slot_count).transpose(1, 0, 2, 3)
    count_blocks = cycle_counts.reshape(blocks, block_rows)

    def forward(block_item):
        pixels, counts = block_item
        tables_now = make_tables(counts, inner_freq, outer_freq, odd_steps)
        real_part, imag_part = analyse(pixels, counts, tables_now, odd_steps)
        return (real_part.reshape(2, block_rows, order_total), imag_part.reshape(2, block_rows, order_total))
    real_part, imag_part = lax.map(forward, (map_blocks, count_blocks))
    real_part = real_part.transpose(1, 0, 2, 3).reshape(2, cycle_total, order_total)
    imag_part = imag_part.transpose(1, 0, 2, 3).reshape(2, cycle_total, order_total)
    folded = jnp.stack([real_part[0] + real_part[1], imag_part[0] + imag_part[1], real_part[0] - real_part[1], imag_part[0] - imag_part[1]], axis=-1).astype(jnp.bfloat16)
    gain = signal_power / (signal_power + noise_power)
    even_mask = jnp.arange(degree_count) % 2 == 0

    def per_order(order_index):
        lam_order = lax.dynamic_index_in_dim(legendre, order_index, 1, keepdims=False)
        folded_order = lax.dynamic_index_in_dim(folded, order_index, 1, keepdims=False)
        sums_full = jnp.dot(folded_order.T, lam_order, preferred_element_type=jnp.float32)
        coef_re = jnp.where(even_mask, sums_full[0], sums_full[2])
        coef_im = jnp.where(even_mask, sums_full[1], sums_full[3])
        start = (M_FIRST + order_index).astype(jnp.int32)
        gain_slice = lax.dynamic_slice_in_dim(gain, start, degree_count)
        filt_re = coef_re * gain_slice
        filt_im = coef_im * gain_slice
        zeros = jnp.zeros_like(filt_re)
        stacked = jnp.stack([jnp.where(even_mask, filt_re, zeros), jnp.where(even_mask, filt_im, zeros), jnp.where(even_mask, zeros, filt_re), jnp.where(even_mask, zeros, filt_im)]).astype(jnp.bfloat16)
        return jnp.dot(lam_order, stacked.T, preferred_element_type=jnp.float32)
    order_modes = lax.map(per_order, jnp.arange(order_total).astype(jnp.int32))
    north_re = order_modes[..., 0] + order_modes[..., 2]
    south_re = order_modes[..., 0] - order_modes[..., 2]
    north_im = order_modes[..., 1] + order_modes[..., 3]
    south_im = order_modes[..., 1] - order_modes[..., 3]
    mode_re = jnp.stack([north_re.T, south_re.T]).astype(jnp.bfloat16)
    mode_im = jnp.stack([north_im.T, south_im.T]).astype(jnp.bfloat16)
    mode_re = mode_re.reshape(2, blocks, block_rows, p_count, q_count * c_count).transpose(1, 0, 2, 3, 4)
    mode_im = mode_im.reshape(2, blocks, block_rows, p_count, q_count * c_count).transpose(1, 0, 2, 3, 4)
    norm_factor = 1.0 / math.sqrt(order_total)

    def backward(block_item):
        block_re, block_im, counts = block_item
        tables_now = make_tables(counts, inner_freq, outer_freq, odd_steps)
        return synthesise(block_re, block_im, counts, tables_now, odd_steps, norm_factor)
    result = lax.map(backward, (mode_re, mode_im, count_blocks))
    return result.transpose(1, 0, 2, 3).reshape(2, cycle_total, slot_count)
```

```python
import math

import jax
import jax.numpy as jnp
from jax import lax
from jax.experimental import pallas as pl
from jax.experimental.pallas import tpu as pltpu
from jax.sharding import PartitionSpec as P

M_FIRST = 2048
N_BLK = 64
N_BAND = 4
R = 8
B = 128
A = 128
A_OWN = A // N_BAND
NR = N_BLK * R
NT = 4096
F32, BF16 = jnp.float32, jnp.bfloat16
MESH = pl.DeviceIdType.MESH
ROUND = 12582912.0
COEFS = (4.442882834158576, -7.308241154915532, 3.606288962930247, -0.8457636193361991, 0.10920579263730913)
DIMS_NT = (((1,), (1,)), ((), ()))


def cos_turns(x, period, inverse):
    whole = (x * inverse + ROUND) - ROUND
    t = (x - whole * period) * inverse
    u = t * t
    p = jnp.full_like(u, COEFS[-1])
    for c in COEFS[-2::-1]:
        p = p * u + c
    s = p * t
    return 1.0 - s * s


def iota(shape, dim):
    return lax.broadcasted_iota(jnp.int32, shape, dim)


def split(x):
    hi = x.astype(BF16)
    return hi, (x - hi.astype(F32)).astype(BF16)


def pixel_table(freq, count, inv_count):
    shape = (B // 8, 8, 128)
    odd = (2 * (iota(shape, 0) * 8 + iota(shape, 1)) + 1).astype(F32)
    quarter = jnp.where(iota((8, 128), 1) >= 64, 0.5 * count, 0.0)
    return cos_turns(odd * freq - quarter, 2.0 * count, 0.5 * inv_count)


def row_parts(first_row, rows, count, inv_count):
    shape = (rows // 8, 8, 128)
    slot = ((iota(shape, 0) * 8 + iota(shape, 1) + first_row) * B).astype(F32)
    near = jnp.where(slot > 0.5 * count, slot - count, slot)
    near = jnp.where(near > 0.5 * count, near - count, near)
    far = near * 1024.0
    far = far - ((far * inv_count + ROUND) - ROUND) * count
    return near, 2.0 * far


def row_table(parts, offset, count, inv_count):
    near, far = parts
    quarter = jnp.where(iota((8, 128), 1) >= 64, 0.25 * count, 0.0)
    return cos_turns(near * offset + (far - quarter), count, inv_count)


def kernel(
    counts, sky, leg, signal, noise, out,
    xs, legv, folded, send1, recv1, send2, recv2, modes, thi, tlo, wtab, wswap, gain, select,
    sky_sem, leg_sem, s1, r1, s2, r2, s3, r3,
):
    blk = lax.axis_index("blk")
    band = lax.axis_index("band")
    sky_copy = pltpu.make_async_copy(sky, xs, sky_sem)
    sky_copy.start()
    leg_copy = pltpu.make_async_copy(leg, legv, leg_sem)
    leg_copy.start()

    barrier = pltpu.get_barrier_semaphore()

    def greet(d, carry):
        pl.semaphore_signal(barrier, inc=1, device_id=(lax.rem(blk + d, N_BLK), band), device_id_type=MESH)
        return carry

    lax.fori_loop(1, N_BLK, greet, 0)
    for e in range(1, N_BAND):
        pl.semaphore_signal(barrier, inc=1, device_id=(blk, lax.rem(band + e, N_BAND)), device_id_type=MESH)

    lane = iota((8, 128), 1)
    own_offset = (lax.rem(lane, 64) * N_BAND + band).astype(F32)
    folded[...] = jnp.zeros_like(folded)
    sky_copy.wait()

    def count_of(r):
        count = jnp.full((8, 128), counts[r], jnp.int32).astype(F32)
        return count, 1.0 / count

    def analyse(r, carry):
        count, inv_count = count_of(r)
        table = pixel_table(own_offset + M_FIRST, count, inv_count).reshape(B, 128)
        t_hi, t_lo = split(table)
        turn = row_table(row_parts(0, A, count, inv_count), own_offset, count, inv_count)
        swapped = pltpu.roll(turn.reshape(A, 128), 64, 1).reshape(A // 8, 8, 128)
        pixels = xs[pl.ds(r, 2 * A, stride=R), :].reshape(2, A // 8, 8, 128)
        shape = (A // 8, 8, 128)
        slot = ((iota(shape, 0) * 8 + iota(shape, 1)) * B + iota(shape, 2)).astype(F32)
        pixels = jnp.where((slot < count)[None], pixels, 0.0).reshape(2 * A, B)
        x_hi, x_lo = split(pixels)
        part = jnp.dot(
            jnp.concatenate([x_hi, x_lo], axis=1), jnp.concatenate([t_hi, t_hi], axis=0), preferred_element_type=F32
        ) + jnp.dot(x_hi, t_lo, preferred_element_type=F32)
        part = part.reshape(2, A // 8, 8, 128)
        first = jnp.sum(part * turn[None], axis=1)
        second = jnp.sum(part * swapped[None], axis=1)
        first = jnp.concatenate([first[0], first[1]], axis=0)
        second = jnp.concatenate([second[0], second[1]], axis=0)
        scale = lax.rsqrt(count)
        scale = scale * (1.5 - 0.5 * count * scale * scale)
        scale2 = jnp.concatenate([scale, scale], axis=0)
        real = (first - pltpu.roll(first, 64, 1)) * scale2
        imag = -(second + pltpu.roll(second, 64, 1)) * scale2
        parts = (
            real[:8] + real[8:],
            imag[:8] + imag[8:],
            real[:8] - real[8:],
            imag[:8] - imag[8:],
        )
        for k, value in enumerate(parts):
            folded[pl.ds(r * 4 + k, 1), :] = jnp.sum(value, axis=0, keepdims=True)
        return carry

    lax.fori_loop(0, R, analyse, 0)

    turned = jnp.transpose(folded[...])[:N_BLK]
    turned_hi = turned.astype(BF16).astype(F32)
    turned_lo = turned - turned_hi
    lanes64 = iota((N_BLK, 128), 1)
    both = jnp.where(lanes64 < 32, turned_hi, jnp.where(lanes64 < 64, pltpu.roll(turned_lo, 32, 1), 0.0))
    send1[...] = both.reshape(N_BLK, 1, 128)

    pl.semaphore_wait(barrier, N_BLK - 1 + N_BAND - 1)

    def exchange(source, target, send_sem, recv_sem):
        def send(d, carry):
            peer = lax.rem(blk + d, N_BLK)
            pltpu.make_async_remote_copy(
                src_ref=source.at[peer],
                dst_ref=target.at[blk],
                send_sem=send_sem,
                recv_sem=recv_sem,
                device_id=(peer, band),
                device_id_type=MESH,
            ).start()
            return carry

        lax.fori_loop(1, N_BLK, send, 0)
        target[blk] = source[blk]
        return pltpu.make_async_remote_copy(
            src_ref=source.at[pl.ds(0, N_BLK - 1)],
            dst_ref=target.at[pl.ds(0, N_BLK - 1)],
            send_sem=send_sem,
            recv_sem=recv_sem,
            device_id=(blk, band),
            device_id_type=MESH,
        )

    done1 = exchange(send1, recv1, s1, r1)

    def prepare(r, carry):
        count, inv_count = count_of(r)
        parts = row_parts(band * A_OWN, A_OWN, count, inv_count)
        for c in range(N_BAND):
            offset = (lax.rem(lane, 64) * N_BAND + c).astype(F32)
            cols = pl.ds(c * 128, 128)
            hi, lo = split(pixel_table(offset + M_FIRST, count, inv_count).reshape(B, 128))
            thi[r, :, cols] = hi
            tlo[r, :, cols] = lo
            turn = row_table(parts, offset, count, inv_count).reshape(A_OWN, 128)
            wtab[r, :, cols] = turn
            wswap[r, :, cols] = pltpu.roll(turn, 64, 1)
        return carry

    lax.fori_loop(0, R, prepare, 0)

    order = blk * N_BAND + band
    low = lax.rem(order, 128)
    power = signal[...]
    rolled = pltpu.roll(power / (power + noise[...]), lax.rem(128 - low, 128), 1)
    gain[...] = rolled
    following = jnp.concatenate([gain[1:, :], gain[:1, :]], axis=0)
    gain[...] = jnp.where(lanes64 < 128 - low, rolled, following)
    first_gain = M_FIRST // 128 + order // 128

    shape = (512, 128)
    for k in range(4):
        select[k * NR : (k + 1) * NR, :] = jnp.where(
            iota(shape, 1) == lax.rem(iota(shape, 0), R) * 4 + k, 1.0, 0.0
        ).astype(BF16)
    comp = iota((8, 128), 0)
    lane_comp = jnp.where(comp < 4, lane, lane - 32)
    pick = jnp.where(
        (lane_comp >= 0) & (lane_comp < 32) & (lax.rem(lane_comp + 32, 4) == lax.rem(comp, 4)), 1.0, 0.0
    ).astype(BF16)

    leg_copy.wait()
    done1.wait_recv()

    shape = (N_BLK, 8, 128)
    here = (iota(shape, 2) < 64) & (lax.rem(iota(shape, 2), 32) // 4 == iota(shape, 1))
    spread = jnp.where(here, jnp.broadcast_to(recv1[...], shape), 0.0).reshape(NR, 128).astype(BF16)
    coeffs = lax.dot_general(pick, spread, DIMS_NT, preferred_element_type=F32).astype(BF16)
    sums = jnp.dot(coeffs, legv[...], preferred_element_type=F32)
    sums = sums + pltpu.roll(sums, 4, 0)
    other = pltpu.roll(sums, 2, 0)
    even = lax.rem(lane, 2) == 0
    upper = lax.rem(comp, 4) >= 2
    sign = jnp.where(upper & ~even, -1.0, 1.0)
    pieces = []
    for k in range(NT // 128):
        cols = slice(k * 128, (k + 1) * 128)
        row = gain[pl.ds(first_gain + k, 1), :]
        value = jnp.where(even ^ upper, sums[:, cols], other[:, cols]) * (row * sign)
        hi = value.astype(BF16).astype(F32)
        pieces.append(jnp.where(comp < 4, hi, value - hi).astype(BF16))
    filtered = jnp.concatenate(pieces, axis=1)
    cycle = lax.dot_general(filtered, legv[...], DIMS_NT, preferred_element_type=F32)
    cycle = cycle + pltpu.roll(cycle, 4, 0)
    shape = (N_BLK, NR)
    own_block = iota(shape, 1) // R == iota(shape, 0)
    blocks = [
        jnp.where(own_block, jnp.broadcast_to(cycle[k : k + 1, :], shape), 0.0).astype(BF16) for k in range(4)
    ]
    rows = jnp.dot(jnp.concatenate(blocks, axis=1), select[...], preferred_element_type=F32)
    send2[...] = rows.reshape(N_BLK, 1, 128)
    done2 = exchange(send2, recv2, s2, r2)
    done2.wait_recv()

    got = recv2[...].reshape(N_BLK, 128)
    got = jnp.transpose(jnp.concatenate([got, got], axis=0))[:32]
    shape = (32, 128)
    is_imag = lax.rem(iota(shape, 0), 2) == 1
    norm = 1.0 / math.sqrt(N_BLK * N_BAND)
    modes[band] = got * jnp.where(is_imag | (iota(shape, 1) >= 64), -norm, norm)
    for e in range(1, N_BAND):
        pltpu.make_async_remote_copy(
            src_ref=modes.at[band],
            dst_ref=modes.at[band],
            send_sem=s3,
            recv_sem=r3,
            device_id=(blk, lax.rem(band + e, N_BAND)),
            device_id_type=MESH,
        ).start()
    done3 = pltpu.make_async_remote_copy(
        src_ref=modes.at[pl.ds(0, N_BAND - 1)],
        dst_ref=modes.at[pl.ds(0, N_BAND - 1)],
        send_sem=s3,
        recv_sem=r3,
        device_id=(blk, band),
        device_id_type=MESH,
    )
    done3.wait_recv()

    def synthesise(r, carry):
        halves = []
        for h in range(2):
            cols = []
            for c in range(N_BAND):
                re = modes[c, pl.ds(r * 4 + 2 * h, 1), :]
                im = modes[c, pl.ds(r * 4 + 2 * h + 1, 1), :]
                at = pl.ds(c * 128, 128)
                cols.append(wtab[r, :, at] * re + wswap[r, :, at] * im)
            halves.append(jnp.concatenate(cols, axis=1))
        z_hi, z_lo = split(jnp.concatenate(halves, axis=0))
        rows = 2 * A_OWN
        t_hi, t_lo = thi[r], tlo[r]
        main = lax.dot_general(jnp.concatenate([z_hi, z_lo], axis=0), t_hi, DIMS_NT, preferred_element_type=F32)
        value = main[:rows] + main[rows:] + lax.dot_general(z_hi, t_lo, DIMS_NT, preferred_element_type=F32)
        shape = (rows, B)
        slot = (lax.rem(iota(shape, 0), A_OWN) + band * A_OWN) * B + iota(shape, 1)
        out[pl.ds(r, rows, stride=R), :] = jnp.where(slot < counts[r], value, 0.0)
        return carry

    lax.fori_loop(0, R, synthesise, 0)
    done1.wait_send()
    done2.wait_send()
    done3.wait_send()


def per_device(sky_map, cycle_counts, legendre, signal_power, noise_power):
    sky = sky_map.reshape(2, R, A, B).transpose(0, 2, 1, 3).reshape(2 * A * R, B)
    leg = legendre.reshape(NR, NT)
    vmem = pl.BlockSpec(memory_space=pltpu.VMEM)
    anywhere = pl.BlockSpec(memory_space=pl.ANY)
    dma = pltpu.SemaphoreType.DMA
    result = pl.pallas_call(
        kernel,
        out_shape=jax.ShapeDtypeStruct((2 * A_OWN * R, B), F32),
        in_specs=[pl.BlockSpec(memory_space=pltpu.SMEM), anywhere, anywhere, vmem, vmem],
        out_specs=vmem,
        scratch_shapes=[
            pltpu.VMEM((2 * A * R, B), F32),
            pltpu.VMEM((NR, NT), BF16),
            pltpu.VMEM((128, 128), F32),
            pltpu.VMEM((N_BLK, 1, 128), F32),
            pltpu.VMEM((N_BLK, 1, 128), F32),
            pltpu.VMEM((N_BLK, 1, 128), F32),
            pltpu.VMEM((N_BLK, 1, 128), F32),
            pltpu.VMEM((N_BAND, 32, 128), F32),
            pltpu.VMEM((R, B, N_BAND * 128), BF16),
            pltpu.VMEM((R, B, N_BAND * 128), BF16),
            pltpu.VMEM((R, A_OWN, N_BAND * 128), F32),
            pltpu.VMEM((R, A_OWN, N_BAND * 128), F32),
            pltpu.VMEM((64, 128), F32),
            pltpu.VMEM((4 * NR, 128), BF16),
            dma, dma, dma, dma, dma, dma, dma, dma,
        ],
        compiler_params=pltpu.CompilerParams(collective_id=0, has_side_effects=True, vmem_limit_bytes=67043328),
    )(cycle_counts, sky, leg, signal_power.reshape(64, 128), noise_power.reshape(64, 128))
    return result.reshape(2, A_OWN, R, B).transpose(0, 2, 1, 3).reshape(2, R, A_OWN * B)


def solution(mesh):
    placed = (P(None, "blk", None), P("blk"), P(None, ("blk", "band"), None), P(), P())
    return jax.shard_map(
        per_device, mesh=mesh, in_specs=placed, out_specs=P(None, "blk", "band"), check_vma=False
    )
```

```python
import math

import jax
import jax.numpy as jnp
from jax import lax
from jax.experimental import pallas as pl
from jax.experimental.pallas import tpu as pltpu
from jax.sharding import PartitionSpec as P

M_FIRST = 2048
N_BLK = 64
N_BAND = 4
R = 8
B = 128
A = 128
A_OWN = A // N_BAND
NR = N_BLK * R
NT = 4096
F32, BF16 = jnp.float32, jnp.bfloat16
MESH = pl.DeviceIdType.MESH
ROUND = 12582912.0
COEFS = (4.442882834158576, -7.308241154915532, 3.606288962930247, -0.8457636193361991, 0.10920579263730913)
DIMS_NT = (((1,), (1,)), ((), ()))


def cos_turns(x, period, inverse):
    whole = (x * inverse + ROUND) - ROUND
    t = (x - whole * period) * inverse
    u = t * t
    p = jnp.full_like(u, COEFS[-1])
    for c in COEFS[-2::-1]:
        p = p * u + c
    s = p * t
    return 1.0 - s * s


def iota(shape, dim):
    return lax.broadcasted_iota(jnp.int32, shape, dim)


def split(x):
    hi = x.astype(BF16)
    return hi, (x - hi.astype(F32)).astype(BF16)


def pixel_table(freq, count, inv_count):
    shape = (B // 8, 8, 128)
    odd = (2 * (iota(shape, 0) * 8 + iota(shape, 1)) + 1).astype(F32)
    quarter = jnp.where(iota((8, 128), 1) >= 64, 0.5 * count, 0.0)
    return cos_turns(odd * freq - quarter, 2.0 * count, 0.5 * inv_count)


def row_parts(first_row, rows, count, inv_count):
    shape = (rows // 8, 8, 128)
    slot = ((iota(shape, 0) * 8 + iota(shape, 1) + first_row) * B).astype(F32)
    near = jnp.where(slot > 0.5 * count, slot - count, slot)
    near = jnp.where(near > 0.5 * count, near - count, near)
    far = near * 1024.0
    far = far - ((far * inv_count + ROUND) - ROUND) * count
    return near, 2.0 * far


def row_table(parts, offset, count, inv_count):
    near, far = parts
    quarter = jnp.where(iota((8, 128), 1) >= 64, 0.25 * count, 0.0)
    return cos_turns(near * offset + (far - quarter), count, inv_count)


def kernel(
    counts_in, sky, leg, signal_in, noise_in, out,
    counts, xs, legv, signal, noise, folded, send1, recv1, send2, recv2, modes, along, across, table, wtab, wswap, gain, select,
    count_sem, sky_sem, leg_sem, signal_sem, noise_sem, s1, r1, s2, r2, s3, r3,
):
    blk = lax.axis_index("blk")
    band = lax.axis_index("band")
    barrier = pltpu.get_barrier_semaphore()

    ys = [lax.rem(lax.div(blk, 16) + d, 4) * 16 for d in range(4)]
    zs = [lax.rem(lax.rem(lax.div(blk, 2), 8) + d, 8) * 2 for d in range(8)]
    cs = [lax.rem(blk + d, 2) for d in range(2)]
    steps = [(y, z, c) for y in range(4) for z in range(8) for c in range(2)][1:]
    steps.sort(key=lambda s: -min(s[0], 4 - s[0]) - min(s[1], 8 - s[1]))
    peers = [ys[y] + zs[z] + cs[c] for y, z, c in steps]

    for peer in peers:
        pl.semaphore_signal(barrier, inc=1, device_id=(peer, band), device_id_type=MESH)
    for e in range(1, N_BAND):
        pl.semaphore_signal(barrier, inc=1, device_id=(blk, lax.rem(band + e, N_BAND)), device_id_type=MESH)
    count_copy = pltpu.make_async_copy(counts_in, counts, count_sem)
    count_copy.start()
    sky_copy = pltpu.make_async_copy(sky, xs, sky_sem)
    sky_copy.start()
    leg_copy = pltpu.make_async_copy(leg, legv, leg_sem)
    leg_copy.start()
    signal_copy = pltpu.make_async_copy(signal_in, signal, signal_sem)
    signal_copy.start()
    noise_copy = pltpu.make_async_copy(noise_in, noise, noise_sem)
    noise_copy.start()

    lane = iota((8, 128), 1)
    own_offset = (lax.rem(lane, 64) * N_BAND + band).astype(F32)
    folded[...] = jnp.zeros_like(folded)
    count_copy.wait()
    sky_copy.wait()

    def count_of(r):
        count = jnp.full((8, 128), counts[r], jnp.int32).astype(F32)
        return count, 1.0 / count

    def analyse(r, carry):
        count, inv_count = count_of(r)
        table = pixel_table(own_offset + M_FIRST, count, inv_count).reshape(B, 128)
        t_hi, t_lo = split(table)
        turn = row_table(row_parts(0, A, count, inv_count), own_offset, count, inv_count)
        swapped = pltpu.roll(turn.reshape(A, 128), 64, 1).reshape(A // 8, 8, 128)
        pixels = xs[pl.ds(r, 2 * A, stride=R), :].reshape(2, A // 8, 8, 128)
        shape = (A // 8, 8, 128)
        slot = ((iota(shape, 0) * 8 + iota(shape, 1)) * B + iota(shape, 2)).astype(F32)
        pixels = jnp.where((slot < count)[None], pixels, 0.0).reshape(2 * A, B)
        x_hi, x_lo = split(pixels)
        part = jnp.dot(
            jnp.concatenate([x_hi, x_lo], axis=1), jnp.concatenate([t_hi, t_hi], axis=0), preferred_element_type=F32
        ) + jnp.dot(x_hi, t_lo, preferred_element_type=F32)
        part = part.reshape(2, A // 8, 8, 128)
        first = jnp.sum(part * turn[None], axis=1)
        second = jnp.sum(part * swapped[None], axis=1)
        first = jnp.concatenate([first[0], first[1]], axis=0)
        second = jnp.concatenate([second[0], second[1]], axis=0)
        scale = lax.rsqrt(count)
        scale = scale * (1.5 - 0.5 * count * scale * scale)
        scale2 = jnp.concatenate([scale, scale], axis=0)
        real = (first - pltpu.roll(first, 64, 1)) * scale2
        imag = -(second + pltpu.roll(second, 64, 1)) * scale2
        parts = (
            real[:8] + real[8:],
            imag[:8] + imag[8:],
            real[:8] - real[8:],
            imag[:8] - imag[8:],
        )
        for k, value in enumerate(parts):
            folded[pl.ds(r * 4 + k, 1), :] = jnp.sum(value, axis=0, keepdims=True)
        return carry

    lax.fori_loop(0, R, analyse, 0)

    turned = jnp.transpose(folded[...])[:N_BLK]
    turned_hi = turned.astype(BF16).astype(F32)
    turned_lo = turned - turned_hi
    lanes64 = iota((N_BLK, 128), 1)
    both = jnp.where(lanes64 < 32, turned_hi, jnp.where(lanes64 < 64, pltpu.roll(turned_lo, 32, 1), 0.0))
    send1[...] = both.reshape(N_BLK, 1, 128)

    pl.semaphore_wait(barrier, N_BLK - 1 + N_BAND - 1)

    def exchange(source, target, send_sem, recv_sem):
        for peer in peers:
            pltpu.make_async_remote_copy(
                src_ref=source.at[peer],
                dst_ref=target.at[blk],
                send_sem=send_sem,
                recv_sem=recv_sem,
                device_id=(peer, band),
                device_id_type=MESH,
            ).start()
        target[blk] = source[blk]
        return pltpu.make_async_remote_copy(
            src_ref=source.at[pl.ds(0, N_BLK - 1)],
            dst_ref=target.at[pl.ds(0, N_BLK - 1)],
            send_sem=send_sem,
            recv_sem=recv_sem,
            device_id=(blk, band),
            device_id_type=MESH,
        )

    done1 = exchange(send1, recv1, s1, r1)

    def prepare(r, carry):
        count, inv_count = count_of(r)
        parts = row_parts(band * A_OWN, A_OWN, count, inv_count)
        for c in range(N_BAND):
            offset = (lax.rem(lane, 64) * N_BAND + c).astype(F32)
            cols = pl.ds(c * 128, 128)
            table[r, :, cols] = pixel_table(offset + M_FIRST, count, inv_count).reshape(B, 128).astype(BF16)
            turn = row_table(parts, offset, count, inv_count).reshape(A_OWN, 128)
            wtab[r, :, cols] = turn
            wswap[r, :, cols] = pltpu.roll(turn, 64, 1)
        return carry

    lax.fori_loop(0, R, prepare, 0)

    order = blk * N_BAND + band
    low = lax.rem(order, 128)
    signal_copy.wait()
    noise_copy.wait()
    power = signal[...]
    rolled = pltpu.roll(power / (power + noise[...]), lax.rem(128 - low, 128), 1)
    gain[...] = rolled
    following = jnp.concatenate([gain[1:, :], gain[:1, :]], axis=0)
    gain[...] = jnp.where(lanes64 < 128 - low, rolled, following)
    first_gain = M_FIRST // 128 + order // 128

    shape = (512, 128)
    for k in range(4):
        select[k * NR : (k + 1) * NR, :] = jnp.where(
            iota(shape, 1) == lax.rem(iota(shape, 0), R) * 4 + k, 1.0, 0.0
        ).astype(BF16)
    comp = iota((8, 128), 0)
    lane_comp = jnp.where(comp < 4, lane, lane - 32)
    pick = jnp.where(
        (lane_comp >= 0) & (lane_comp < 32) & (lax.rem(lane_comp + 32, 4) == lax.rem(comp, 4)), 1.0, 0.0
    ).astype(BF16)

    leg_copy.wait()
    done1.wait_recv()

    shape = (N_BLK, 8, 128)
    here = (iota(shape, 2) < 64) & (lax.rem(iota(shape, 2), 32) // 4 == iota(shape, 1))
    spread = jnp.where(here, jnp.broadcast_to(recv1[...], shape), 0.0).reshape(NR, 128).astype(BF16)
    coeffs = lax.dot_general(pick, spread, DIMS_NT, preferred_element_type=F32).astype(BF16)
    sums = jnp.dot(coeffs, legv[...], preferred_element_type=F32)
    sums = sums + pltpu.roll(sums, 4, 0)
    other = pltpu.roll(sums, 2, 0)
    even = lax.rem(lane, 2) == 0
    upper = lax.rem(comp, 4) >= 2
    sign = jnp.where(upper & ~even, -1.0, 1.0)
    pieces = []
    for k in range(NT // 128):
        cols = slice(k * 128, (k + 1) * 128)
        row = gain[pl.ds(first_gain + k, 1), :]
        value = jnp.where(even ^ upper, sums[:, cols], other[:, cols]) * (row * sign)
        hi = value.astype(BF16).astype(F32)
        pieces.append(jnp.where(comp < 4, hi, value - hi).astype(BF16))
    filtered = jnp.concatenate(pieces, axis=1)
    cycle = lax.dot_general(filtered, legv[...], DIMS_NT, preferred_element_type=F32)
    cycle = cycle + pltpu.roll(cycle, 4, 0)
    shape = (N_BLK, NR)
    own_block = iota(shape, 1) // R == iota(shape, 0)
    blocks = [
        jnp.where(own_block, jnp.broadcast_to(cycle[k : k + 1, :], shape), 0.0).astype(BF16) for k in range(4)
    ]
    rows = jnp.dot(jnp.concatenate(blocks, axis=1), select[...], preferred_element_type=F32)
    send2[...] = rows.reshape(N_BLK, 1, 128)
    done2 = exchange(send2, recv2, s2, r2)
    done2.wait_recv()

    got = jnp.transpose(jnp.concatenate([recv2[...].reshape(N_BLK, 128)] * 2, axis=0))[:32]
    got = got.reshape(16, 2, 128)
    shape = (16, 128)
    modes[band] = jnp.where(iota(shape, 1) < 64, got[:, 0], got[:, 1]).astype(BF16)
    for e in range(1, N_BAND):
        pltpu.make_async_remote_copy(
            src_ref=modes.at[band],
            dst_ref=modes.at[band],
            send_sem=s3,
            recv_sem=r3,
            device_id=(blk, lax.rem(band + e, N_BAND)),
            device_id_type=MESH,
        ).start()
    done3 = pltpu.make_async_remote_copy(
        src_ref=modes.at[pl.ds(0, N_BAND - 1)],
        dst_ref=modes.at[pl.ds(0, N_BAND - 1)],
        send_sem=s3,
        recv_sem=r3,
        device_id=(blk, band),
        device_id_type=MESH,
    )
    done3.wait_recv()

    shape = (N_BAND, 16, 128)
    norm = 1.0 / math.sqrt(N_BLK * N_BAND)
    got = modes[...].astype(F32) * norm
    turned = pltpu.roll(got, 64, 2)
    left = iota(shape, 2) < 64
    along[...] = jnp.where(left, got, -turned)
    across[...] = jnp.where(left, -turned, -got)

    def synthesise(r, carry):
        halves = []
        for h in range(2):
            cols = []
            for c in range(N_BAND):
                row = pl.ds(r * 2 + h, 1)
                at = pl.ds(c * 128, 128)
                cols.append(wtab[r, :, at] * along[c, row, :] + wswap[r, :, at] * across[c, row, :])
            halves.append(jnp.concatenate(cols, axis=1))
        z = jnp.concatenate(halves, axis=0).astype(BF16)
        value = lax.dot_general(z, table[r], DIMS_NT, preferred_element_type=F32)
        shape = (2 * A_OWN, B)
        slot = (lax.rem(iota(shape, 0), A_OWN) + band * A_OWN) * B + iota(shape, 1)
        out[pl.ds(r, 2 * A_OWN, stride=R), :] = jnp.where(slot < counts[r], value, 0.0)
        return carry

    lax.fori_loop(0, R, synthesise, 0)
    done1.wait_send()
    done2.wait_send()
    done3.wait_send()


def per_device(sky_map, cycle_counts, legendre, signal_power, noise_power):
    sky = sky_map.reshape(2, R, A, B).transpose(0, 2, 1, 3).reshape(2 * A * R, B)
    leg = legendre.reshape(NR, NT)
    vmem = pl.BlockSpec(memory_space=pltpu.VMEM)
    anywhere = pl.BlockSpec(memory_space=pl.ANY)
    dma = pltpu.SemaphoreType.DMA
    result = pl.pallas_call(
        kernel,
        out_shape=jax.ShapeDtypeStruct((2 * A_OWN * R, B), F32),
        in_specs=[anywhere] * 5,
        out_specs=vmem,
        scratch_shapes=[
            pltpu.SMEM((R,), jnp.int32),
            pltpu.VMEM((2 * A * R, B), F32),
            pltpu.VMEM((NR, NT), BF16),
            pltpu.VMEM((64, 128), F32),
            pltpu.VMEM((64, 128), F32),
            pltpu.VMEM((128, 128), F32),
            pltpu.VMEM((N_BLK, 1, 128), F32),
            pltpu.VMEM((N_BLK, 1, 128), F32),
            pltpu.VMEM((N_BLK, 1, 128), F32),
            pltpu.VMEM((N_BLK, 1, 128), F32),
            pltpu.VMEM((N_BAND, 16, 128), BF16),
            pltpu.VMEM((N_BAND, 16, 128), F32),
            pltpu.VMEM((N_BAND, 16, 128), F32),
            pltpu.VMEM((R, B, N_BAND * 128), BF16),
            pltpu.VMEM((R, A_OWN, N_BAND * 128), F32),
            pltpu.VMEM((R, A_OWN, N_BAND * 128), F32),
            pltpu.VMEM((64, 128), F32),
            pltpu.VMEM((4 * NR, 128), BF16),
            *([dma] * 11),
        ],
        compiler_params=pltpu.CompilerParams(collective_id=0, has_side_effects=True, vmem_limit_bytes=67043328),
    )(cycle_counts, sky, leg, signal_power.reshape(64, 128), noise_power.reshape(64, 128))
    return result.reshape(2, A_OWN, R, B).transpose(0, 2, 1, 3).reshape(2, R, A_OWN * B)


def solution(mesh):
    placed = (P(None, "blk", None), P("blk"), P(None, ("blk", "band"), None), P(), P())
    return jax.shard_map(
        per_device, mesh=mesh, in_specs=placed, out_specs=P(None, "blk", "band"), check_vma=False
    )
```

```python
import math

import jax
import jax.numpy as jnp
from jax import lax
from jax.experimental import pallas as pl
from jax.experimental.pallas import tpu as pltpu
from jax.sharding import PartitionSpec as P

M_FIRST = 2048
N_BLK = 64
N_BAND = 4
R = 8
B = 128
A = 128
A_OWN = A // N_BAND
NR = N_BLK * R
NT = 4096
F32, BF16 = jnp.float32, jnp.bfloat16
MESH = pl.DeviceIdType.MESH
ROUND = 12582912.0
COEFS = (4.442882834158576, -7.308241154915532, 3.606288962930247, -0.8457636193361991, 0.10920579263730913)
DIMS_NT = (((1,), (1,)), ((), ()))


def cos_turns(x, period, inverse):
    whole = (x * inverse + ROUND) - ROUND
    t = (x - whole * period) * inverse
    u = t * t
    p = jnp.full_like(u, COEFS[-1])
    for c in COEFS[-2::-1]:
        p = p * u + c
    s = p * t
    return 1.0 - s * s


def iota(shape, dim):
    return lax.broadcasted_iota(jnp.int32, shape, dim)


def split(x):
    hi = x.astype(BF16)
    return hi, (x - hi.astype(F32)).astype(BF16)


def pixel_table(freq, count, inv_count):
    shape = (B // 8, 8, 128)
    odd = (2 * (iota(shape, 0) * 8 + iota(shape, 1)) + 1).astype(F32)
    quarter = jnp.where(iota((8, 128), 1) >= 64, 0.5 * count, 0.0)
    return cos_turns(odd * freq - quarter, 2.0 * count, 0.5 * inv_count)


def order_table(c, sines, count, inv_count):
    shape = (8, 8, 128)
    row = iota(shape, 0) * 8 + iota(shape, 1)
    freq = (row * N_BAND + (M_FIRST + c)).astype(F32)
    odd = (2 * iota((8, 128), 1) + 1).astype(F32)
    x = freq * odd
    return cos_turns(x + 0.5 * count if sines else x, 2.0 * count, 0.5 * inv_count)


def row_parts(first_row, rows, count, inv_count):
    shape = (rows // 8, 8, 128)
    slot = ((iota(shape, 0) * 8 + iota(shape, 1) + first_row) * B).astype(F32)
    near = jnp.where(slot > 0.5 * count, slot - count, slot)
    near = jnp.where(near > 0.5 * count, near - count, near)
    far = near * 1024.0
    far = far - ((far * inv_count + ROUND) - ROUND) * count
    return near, 2.0 * far


def row_table(parts, offset, count, inv_count, quarter):
    near, far = parts
    return cos_turns(near * offset + (far - quarter), count, inv_count)


def kernel(
    counts_in, sky, leg, signal_in, noise_in, out,
    counts, xs, legv, signal, noise, folded, send1, recv1, send2, recv2, modes, table, wcos, wsin, gain, select,
    count_sem, sky_sem, leg_sem, signal_sem, noise_sem, s1, r1, s2, r2,
):
    blk = lax.axis_index("blk")
    band = lax.axis_index("band")
    barrier = pltpu.get_barrier_semaphore()

    ys = [lax.rem(lax.div(blk, 16) + d, 4) * 16 for d in range(4)]
    zs = [lax.rem(lax.rem(lax.div(blk, 2), 8) + d, 8) * 2 for d in range(8)]
    cs = [lax.rem(blk + d, 2) for d in range(2)]
    steps = [(y, z, c) for y in range(4) for z in range(8) for c in range(2)][1:]
    steps.sort(key=lambda s: -min(s[0], 4 - s[0]) - min(s[1], 8 - s[1]))
    everyone = [(x, s) for x in range(N_BAND) for s in [(0, 0, 0)] + steps][1:]
    everyone.sort(key=lambda t: -min(t[0], 4 - t[0]) - min(t[1][0], 4 - t[1][0]) - min(t[1][1], 8 - t[1][1]))
    bands = [lax.rem(band + x, N_BAND) for x in range(N_BAND)]
    everyone = [(ys[y] + zs[z] + cs[c], bands[x]) for x, (y, z, c) in everyone]
    peers = [ys[y] + zs[z] + cs[c] for y, z, c in steps]

    for peer in peers:
        pl.semaphore_signal(barrier, inc=1, device_id=(peer, band), device_id_type=MESH)
    for e in range(1, N_BAND):
        pl.semaphore_signal(barrier, inc=1, device_id=(blk, lax.rem(band + e, N_BAND)), device_id_type=MESH)
    count_copy = pltpu.make_async_copy(counts_in, counts, count_sem)
    count_copy.start()
    sky_copy = pltpu.make_async_copy(sky, xs, sky_sem)
    sky_copy.start()
    leg_copy = pltpu.make_async_copy(leg, legv, leg_sem)
    leg_copy.start()
    signal_copy = pltpu.make_async_copy(signal_in, signal, signal_sem)
    signal_copy.start()
    noise_copy = pltpu.make_async_copy(noise_in, noise, noise_sem)
    noise_copy.start()

    lane = iota((8, 128), 1)
    own_offset = (lax.rem(lane, 64) * N_BAND + band).astype(F32)
    folded[...] = jnp.zeros_like(folded)
    count_copy.wait()
    sky_copy.wait()

    def count_of(r):
        count = jnp.full((8, 128), counts[r], jnp.int32).astype(F32)
        return count, 1.0 / count

    def analyse(r, carry):
        count, inv_count = count_of(r)
        table = pixel_table(own_offset + M_FIRST, count, inv_count).reshape(B, 128)
        t_hi, t_lo = split(table)
        quarter = jnp.where(lane >= 64, 0.25 * count, 0.0)
        turn = row_table(row_parts(0, A, count, inv_count), own_offset, count, inv_count, quarter)
        swapped = pltpu.roll(turn.reshape(A, 128), 64, 1).reshape(A // 8, 8, 128)
        pixels = xs[pl.ds(r, 2 * A, stride=R), :].reshape(2, A // 8, 8, 128)
        shape = (A // 8, 8, 128)
        slot = ((iota(shape, 0) * 8 + iota(shape, 1)) * B + iota(shape, 2)).astype(F32)
        pixels = jnp.where((slot < count)[None], pixels, 0.0).reshape(2 * A, B)
        x_hi, x_lo = split(pixels)
        part = jnp.dot(
            jnp.concatenate([x_hi, x_lo], axis=1), jnp.concatenate([t_hi, t_hi], axis=0), preferred_element_type=F32
        ) + jnp.dot(x_hi, t_lo, preferred_element_type=F32)
        part = part.reshape(2, A // 8, 8, 128)
        first = jnp.sum(part * turn[None], axis=1)
        second = jnp.sum(part * swapped[None], axis=1)
        first = jnp.concatenate([first[0], first[1]], axis=0)
        second = jnp.concatenate([second[0], second[1]], axis=0)
        scale = lax.rsqrt(count)
        scale = scale * (1.5 - 0.5 * count * scale * scale)
        scale2 = jnp.concatenate([scale, scale], axis=0)
        real = (first - pltpu.roll(first, 64, 1)) * scale2
        imag = -(second + pltpu.roll(second, 64, 1)) * scale2
        parts = (
            real[:8] + real[8:],
            imag[:8] + imag[8:],
            real[:8] - real[8:],
            imag[:8] - imag[8:],
        )
        for k, value in enumerate(parts):
            folded[pl.ds(r * 4 + k, 1), :] = jnp.sum(value, axis=0, keepdims=True)
        return carry

    lax.fori_loop(0, R, analyse, 0)

    turned = jnp.transpose(folded[...])[:N_BLK]
    turned_hi = turned.astype(BF16).astype(F32)
    turned_lo = turned - turned_hi
    lanes64 = iota((N_BLK, 128), 1)
    both = jnp.where(lanes64 < 32, turned_hi, jnp.where(lanes64 < 64, pltpu.roll(turned_lo, 32, 1), 0.0))
    send1[...] = both.reshape(N_BLK, 1, 128)

    pl.semaphore_wait(barrier, N_BLK - 1 + N_BAND - 1)

    def exchange(source, target, send_sem, recv_sem):
        for peer in peers:
            pltpu.make_async_remote_copy(
                src_ref=source.at[peer],
                dst_ref=target.at[blk],
                send_sem=send_sem,
                recv_sem=recv_sem,
                device_id=(peer, band),
                device_id_type=MESH,
            ).start()
        target[blk] = source[blk]
        return pltpu.make_async_remote_copy(
            src_ref=source.at[pl.ds(0, N_BLK - 1)],
            dst_ref=target.at[pl.ds(0, N_BLK - 1)],
            send_sem=send_sem,
            recv_sem=recv_sem,
            device_id=(blk, band),
            device_id_type=MESH,
        )

    done1 = exchange(send1, recv1, s1, r1)

    def prepare(r, carry):
        count, inv_count = count_of(r)
        parts = row_parts(band * A_OWN, A_OWN, count, inv_count)
        for c in range(N_BAND):
            table[r, pl.ds(c * 64, 64), :] = order_table(c, False, count, inv_count).reshape(64, B).astype(BF16)
            table[r, pl.ds(256 + c * 64, 64), :] = order_table(c, True, count, inv_count).reshape(64, B).astype(BF16)
        for p in range(2):
            offset = (lax.rem(lane, 64) * N_BAND + lax.div(lane, 64) + 2 * p).astype(F32)
            cols = pl.ds(p * 128, 128)
            wcos[r, :, cols] = row_table(parts, offset, count, inv_count, 0.0).reshape(A_OWN, 128)
            wsin[r, :, cols] = row_table(parts, offset, count, inv_count, 0.25 * count).reshape(A_OWN, 128)
        return carry

    lax.fori_loop(0, R, prepare, 0)

    order = blk * N_BAND + band
    low = lax.rem(order, 128)
    signal_copy.wait()
    noise_copy.wait()
    power = signal[...]
    rolled = pltpu.roll(power / (power + noise[...]), lax.rem(128 - low, 128), 1)
    gain[...] = rolled
    following = jnp.concatenate([gain[1:, :], gain[:1, :]], axis=0)
    gain[...] = jnp.where(lanes64 < 128 - low, rolled, following)
    first_gain = M_FIRST // 128 + order // 128

    shape = (512, 128)
    for k in range(4):
        select[k * NR : (k + 1) * NR, :] = jnp.where(
            iota(shape, 1) == lax.rem(iota(shape, 0), R) * 4 + k, 1.0, 0.0
        ).astype(BF16)
    comp = iota((8, 128), 0)
    lane_comp = jnp.where(comp < 4, lane, lane - 32)
    pick = jnp.where(
        (lane_comp >= 0) & (lane_comp < 32) & (lax.rem(lane_comp + 32, 4) == lax.rem(comp, 4)), 1.0, 0.0
    ).astype(BF16)

    leg_copy.wait()
    done1.wait_recv()

    shape = (N_BLK, 8, 128)
    here = (iota(shape, 2) < 64) & (lax.rem(iota(shape, 2), 32) // 4 == iota(shape, 1))
    spread = jnp.where(here, jnp.broadcast_to(recv1[...], shape), 0.0).reshape(NR, 128).astype(BF16)
    coeffs = lax.dot_general(pick, spread, DIMS_NT, preferred_element_type=F32).astype(BF16)
    sums = jnp.dot(coeffs, legv[...], preferred_element_type=F32)
    sums = sums + pltpu.roll(sums, 4, 0)
    other = pltpu.roll(sums, 2, 0)
    even = lax.rem(lane, 2) == 0
    upper = lax.rem(comp, 4) >= 2
    sign = jnp.where(upper & ~even, -1.0, 1.0)
    pieces = []
    for k in range(NT // 128):
        cols = slice(k * 128, (k + 1) * 128)
        row = gain[pl.ds(first_gain + k, 1), :]
        value = jnp.where(even ^ upper, sums[:, cols], other[:, cols]) * (row * sign)
        hi = value.astype(BF16).astype(F32)
        pieces.append(jnp.where(comp < 4, hi, value - hi).astype(BF16))
    filtered = jnp.concatenate(pieces, axis=1)
    cycle = lax.dot_general(filtered, legv[...], DIMS_NT, preferred_element_type=F32)
    cycle = cycle + pltpu.roll(cycle, 4, 0)
    shape = (N_BLK, NR)
    own_block = iota(shape, 1) // R == iota(shape, 0)
    blocks = [
        jnp.where(own_block, jnp.broadcast_to(cycle[k : k + 1, :], shape), 0.0).astype(BF16) for k in range(4)
    ]
    rows = jnp.dot(jnp.concatenate(blocks, axis=1), select[...], preferred_element_type=F32)
    send2[...] = rows.reshape(N_BLK, 1, 128)
    for peer, to in everyone:
        pltpu.make_async_remote_copy(
            src_ref=send2.at[peer],
            dst_ref=recv2.at[band * N_BLK + blk],
            send_sem=s2,
            recv_sem=r2,
            device_id=(peer, to),
            device_id_type=MESH,
        ).start()
    recv2[band * N_BLK + blk] = send2[blk]
    done2 = pltpu.make_async_remote_copy(
        src_ref=recv2.at[pl.ds(0, N_BLK * N_BAND - 1)],
        dst_ref=recv2.at[pl.ds(0, N_BLK * N_BAND - 1)],
        send_sem=s2,
        recv_sem=r2,
        device_id=(blk, band),
        device_id_type=MESH,
    )
    done2.wait_recv()

    norm = 1.0 / math.sqrt(N_BLK * N_BAND)
    for p in range(2):
        got = jnp.transpose(recv2[pl.ds(p * 128, 128)].reshape(128, 128))[:32]
        modes[:, p * 128 : (p + 1) * 128] = got * norm

    def synthesise(r, carry):
        halves = []
        for h in range(2):
            re = modes[pl.ds(r * 4 + 2 * h, 1), :]
            im = modes[pl.ds(r * 4 + 2 * h + 1, 1), :]
            cosines, sines = wcos[r], wsin[r]
            halves.append(jnp.concatenate([cosines * re - sines * im, sines * re + cosines * im], axis=1))
        z = jnp.concatenate(halves, axis=0).astype(BF16)
        value = jnp.dot(z, table[r], preferred_element_type=F32)
        shape = (2 * A_OWN, B)
        slot = (lax.rem(iota(shape, 0), A_OWN) + band * A_OWN) * B + iota(shape, 1)
        out[pl.ds(r, 2 * A_OWN, stride=R), :] = jnp.where(slot < counts[r], value, 0.0)
        return carry

    lax.fori_loop(0, R, synthesise, 0, unroll=True)
    done1.wait_send()
    done2.wait_send()


def per_device(sky_map, cycle_counts, legendre, signal_power, noise_power):
    sky = sky_map.reshape(2, R, A, B).transpose(0, 2, 1, 3).reshape(2 * A * R, B)
    leg = legendre.reshape(NR, NT)
    vmem = pl.BlockSpec(memory_space=pltpu.VMEM)
    anywhere = pl.BlockSpec(memory_space=pltpu.HBM)
    dma = pltpu.SemaphoreType.DMA
    result = pl.pallas_call(
        kernel,
        out_shape=jax.ShapeDtypeStruct((2 * A_OWN * R, B), F32),
        in_specs=[anywhere] * 5,
        out_specs=vmem,
        scratch_shapes=[
            pltpu.SMEM((R,), jnp.int32),
            pltpu.VMEM((2 * A * R, B), F32),
            pltpu.VMEM((NR, NT), BF16),
            pltpu.VMEM((64, 128), F32),
            pltpu.VMEM((64, 128), F32),
            pltpu.VMEM((128, 128), F32),
            pltpu.VMEM((N_BLK, 1, 128), F32),
            pltpu.VMEM((N_BLK, 1, 128), F32),
            pltpu.VMEM((N_BLK, 1, 128), F32),
            pltpu.VMEM((N_BAND * N_BLK, 1, 128), F32),
            pltpu.VMEM((32, N_BAND * 64), F32),
            pltpu.VMEM((R, N_BAND * 128, B), BF16),
            pltpu.VMEM((R, A_OWN, N_BAND * 64), F32),
            pltpu.VMEM((R, A_OWN, N_BAND * 64), F32),
            pltpu.VMEM((64, 128), F32),
            pltpu.VMEM((4 * NR, 128), BF16),
            *([dma] * 9),
        ],
        compiler_params=pltpu.CompilerParams(collective_id=0, has_side_effects=True, vmem_limit_bytes=67043328),
    )(cycle_counts, sky, leg, signal_power.reshape(64, 128), noise_power.reshape(64, 128))
    return result.reshape(2, A_OWN, R, B).transpose(0, 2, 1, 3).reshape(2, R, A_OWN * B)


def solution(mesh):
    placed = (P(None, "blk", None), P("blk"), P(None, ("blk", "band"), None), P(), P())
    return jax.shard_map(
        per_device, mesh=mesh, in_specs=placed, out_specs=P(None, "blk", "band"), check_vma=False
    )
```

```python
import math

import jax
import jax.numpy as jnp
from jax import lax
from jax.experimental import pallas as pl
from jax.experimental.pallas import tpu as pltpu
from jax.sharding import PartitionSpec as P

M_FIRST = 2048
N_BLK = 64
N_BAND = 4
R = 8
B = 128
A = 128
A_OWN = A // N_BAND
NR = N_BLK * R
NT = 4096
F32, BF16 = jnp.float32, jnp.bfloat16
MESH = pl.DeviceIdType.MESH
ROUND = 12582912.0
COEFS = (4.442882834158576, -7.308241154915532, 3.606288962930247, -0.8457636193361991, 0.10920579263730913)
DIMS_NT = (((1,), (1,)), ((), ()))


def cos_turns(x, period, inverse):
    whole = (x * inverse + ROUND) - ROUND
    t = (x - whole * period) * inverse
    u = t * t
    p = jnp.full_like(u, COEFS[-1])
    for c in COEFS[-2::-1]:
        p = p * u + c
    s = p * t
    return 1.0 - s * s


def iota(shape, dim):
    return lax.broadcasted_iota(jnp.int32, shape, dim)


def split(x):
    hi = x.astype(BF16)
    return hi, (x - hi.astype(F32)).astype(BF16)


def pixel_table(freq, count, inv_count):
    shape = (B // 8, 8, 128)
    odd = (2 * (iota(shape, 0) * 8 + iota(shape, 1)) + 1).astype(F32)
    quarter = jnp.where(iota((8, 128), 1) >= 64, 0.5 * count, 0.0)
    return cos_turns(odd * freq - quarter, 2.0 * count, 0.5 * inv_count)


def order_table(c, sines, count, inv_count):
    shape = (8, 8, 128)
    row = iota(shape, 0) * 8 + iota(shape, 1)
    freq = (row * N_BAND + (M_FIRST + c)).astype(F32)
    odd = (2 * iota((8, 128), 1) + 1).astype(F32)
    x = freq * odd
    return cos_turns(x + 0.5 * count if sines else x, 2.0 * count, 0.5 * inv_count)


def row_parts(first_row, rows, count, inv_count):
    shape = (rows // 8, 8, 128)
    slot = ((iota(shape, 0) * 8 + iota(shape, 1) + first_row) * B).astype(F32)
    near = jnp.where(slot > 0.5 * count, slot - count, slot)
    near = jnp.where(near > 0.5 * count, near - count, near)
    far = near * 1024.0
    far = far - ((far * inv_count + ROUND) - ROUND) * count
    return near, 2.0 * far


def row_table(parts, offset, count, inv_count, quarter):
    near, far = parts
    return cos_turns(near * offset + (far - quarter), count, inv_count)


def kernel(
    counts_in, sky, leg, signal_in, noise_in, out,
    counts, xs, legv, leg_turned, signal, noise, folded, send1, recv1, send2, recv2, modes, table, wcos, wsin, gain, select,
    count_sem, sky_sem, leg_sem, signal_sem, noise_sem, s1, r1, s2, r2,
):
    blk = lax.axis_index("blk")
    band = lax.axis_index("band")
    barrier = pltpu.get_barrier_semaphore()

    ys = [lax.rem(lax.div(blk, 16) + d, 4) * 16 for d in range(4)]
    zs = [lax.rem(lax.rem(lax.div(blk, 2), 8) + d, 8) * 2 for d in range(8)]
    cs = [lax.rem(blk + d, 2) for d in range(2)]
    steps = [(y, z, c) for y in range(4) for z in range(8) for c in range(2)][1:]
    steps.sort(key=lambda s: -min(s[0], 4 - s[0]) - min(s[1], 8 - s[1]))
    everyone = [(x, s) for x in range(N_BAND) for s in [(0, 0, 0)] + steps][1:]
    everyone.sort(key=lambda t: -min(t[0], 4 - t[0]) - min(t[1][0], 4 - t[1][0]) - min(t[1][1], 8 - t[1][1]))
    bands = [lax.rem(band + x, N_BAND) for x in range(N_BAND)]
    everyone = [(ys[y] + zs[z] + cs[c], bands[x]) for x, (y, z, c) in everyone]
    peers = [ys[y] + zs[z] + cs[c] for y, z, c in steps]

    for peer in peers:
        pl.semaphore_signal(barrier, inc=1, device_id=(peer, band), device_id_type=MESH)
    for e in range(1, N_BAND):
        pl.semaphore_signal(barrier, inc=1, device_id=(blk, lax.rem(band + e, N_BAND)), device_id_type=MESH)
    count_copy = pltpu.make_async_copy(counts_in, counts, count_sem)
    count_copy.start()
    sky_copy = pltpu.make_async_copy(sky, xs, sky_sem)
    sky_copy.start()
    leg_copy = pltpu.make_async_copy(leg, legv, leg_sem)
    leg_copy.start()
    signal_copy = pltpu.make_async_copy(signal_in, signal, signal_sem)
    signal_copy.start()
    noise_copy = pltpu.make_async_copy(noise_in, noise, noise_sem)
    noise_copy.start()

    lane = iota((8, 128), 1)
    own_offset = (lax.rem(lane, 64) * N_BAND + band).astype(F32)
    folded[...] = jnp.zeros_like(folded)
    count_copy.wait()
    sky_copy.wait()

    def count_of(r):
        count = jnp.full((8, 128), counts[r], jnp.int32).astype(F32)
        return count, 1.0 / count

    def analyse(r, carry):
        count, inv_count = count_of(r)
        table = pixel_table(own_offset + M_FIRST, count, inv_count).reshape(B, 128)
        t_hi, t_lo = split(table)
        quarter = jnp.where(lane >= 64, 0.25 * count, 0.0)
        turn = row_table(row_parts(0, A, count, inv_count), own_offset, count, inv_count, quarter)
        swapped = pltpu.roll(turn.reshape(A, 128), 64, 1).reshape(A // 8, 8, 128)
        pixels = xs[pl.ds(r, 2 * A, stride=R), :].reshape(2, A // 8, 8, 128)
        shape = (A // 8, 8, 128)
        slot = ((iota(shape, 0) * 8 + iota(shape, 1)) * B + iota(shape, 2)).astype(F32)
        pixels = jnp.where((slot < count)[None], pixels, 0.0).reshape(2 * A, B)
        x_hi, x_lo = split(pixels)
        part = jnp.dot(
            jnp.concatenate([x_hi, x_lo], axis=1), jnp.concatenate([t_hi, t_hi], axis=0), preferred_element_type=F32
        ) + jnp.dot(x_hi, t_lo, preferred_element_type=F32)
        part = part.reshape(2, A // 8, 8, 128)
        first = jnp.sum(part * turn[None], axis=1)
        second = jnp.sum(part * swapped[None], axis=1)
        first = jnp.concatenate([first[0], first[1]], axis=0)
        second = jnp.concatenate([second[0], second[1]], axis=0)
        scale = lax.rsqrt(count)
        scale = scale * (1.5 - 0.5 * count * scale * scale)
        scale2 = jnp.concatenate([scale, scale], axis=0)
        real = (first - pltpu.roll(first, 64, 1)) * scale2
        imag = -(second + pltpu.roll(second, 64, 1)) * scale2
        parts = (
            real[:8] + real[8:],
            imag[:8] + imag[8:],
            real[:8] - real[8:],
            imag[:8] - imag[8:],
        )
        for k, value in enumerate(parts):
            folded[pl.ds(r * 4 + k, 1), :] = jnp.sum(value, axis=0, keepdims=True)
        return carry

    lax.fori_loop(0, R, analyse, 0)

    turned = jnp.transpose(folded[...])[:N_BLK]
    turned_hi = turned.astype(BF16).astype(F32)
    turned_lo = turned - turned_hi
    lanes64 = iota((N_BLK, 128), 1)
    both = jnp.where(lanes64 < 32, turned_hi, jnp.where(lanes64 < 64, pltpu.roll(turned_lo, 32, 1), 0.0))
    send1[...] = both.reshape(N_BLK, 1, 128)

    pl.semaphore_wait(barrier, N_BLK - 1 + N_BAND - 1)

    def exchange(source, target, send_sem, recv_sem):
        for peer in peers:
            pltpu.make_async_remote_copy(
                src_ref=source.at[peer],
                dst_ref=target.at[blk],
                send_sem=send_sem,
                recv_sem=recv_sem,
                device_id=(peer, band),
                device_id_type=MESH,
            ).start()
        target[blk] = source[blk]
        return pltpu.make_async_remote_copy(
            src_ref=source.at[pl.ds(0, N_BLK - 1)],
            dst_ref=target.at[pl.ds(0, N_BLK - 1)],
            send_sem=send_sem,
            recv_sem=recv_sem,
            device_id=(blk, band),
            device_id_type=MESH,
        )

    done1 = exchange(send1, recv1, s1, r1)

    def prepare(r, carry):
        count, inv_count = count_of(r)
        parts = row_parts(band * A_OWN, A_OWN, count, inv_count)
        for c in range(N_BAND):
            table[r, pl.ds(c * 64, 64), :] = order_table(c, False, count, inv_count).reshape(64, B).astype(BF16)
            table[r, pl.ds(256 + c * 64, 64), :] = order_table(c, True, count, inv_count).reshape(64, B).astype(BF16)
        for p in range(2):
            offset = (lax.rem(lane, 64) * N_BAND + lax.div(lane, 64) + 2 * p).astype(F32)
            cols = pl.ds(p * 128, 128)
            wcos[r, :, cols] = row_table(parts, offset, count, inv_count, 0.0).reshape(A_OWN, 128)
            wsin[r, :, cols] = row_table(parts, offset, count, inv_count, 0.25 * count).reshape(A_OWN, 128)
        return carry

    lax.fori_loop(0, R, prepare, 0)

    leg_copy.wait()

    def turn_legendre(k, carry):
        cols = pl.ds(pl.multiple_of(k * 128, 128), 128)
        leg_turned[cols, :] = jnp.transpose(legv[:, cols])
        return carry

    lax.fori_loop(0, NT // 128, turn_legendre, 0, unroll=2)

    order = blk * N_BAND + band
    low = lax.rem(order, 128)
    signal_copy.wait()
    noise_copy.wait()
    power = signal[...]
    rolled = pltpu.roll(power / (power + noise[...]), lax.rem(128 - low, 128), 1)
    gain[...] = rolled
    following = jnp.concatenate([gain[1:, :], gain[:1, :]], axis=0)
    gain[...] = jnp.where(lanes64 < 128 - low, rolled, following)
    first_gain = M_FIRST // 128 + order // 128

    def permute(k, carry):
        rows = pl.ds(pl.multiple_of(k * 64, 64), 64)
        source = iota((64, NR), 0) + k * 64
        column = iota((64, NR), 1)
        select[rows, :] = jnp.where(lax.rem(column, N_BLK) * R + column // N_BLK == source, 1.0, 0.0).astype(BF16)
        return carry

    lax.fori_loop(0, NR // 64, permute, 0)
    comp = iota((8, 128), 0)
    lane_comp = jnp.where(comp < 4, lane, lane - 32)
    pick = jnp.where(
        (lane_comp >= 0) & (lane_comp < 32) & (lax.rem(lane_comp + 32, 4) == lax.rem(comp, 4)), 1.0, 0.0
    ).astype(BF16)

    done1.wait_recv()

    shape = (N_BLK, 8, 128)
    here = (iota(shape, 2) < 64) & (lax.rem(iota(shape, 2), 32) // 4 == iota(shape, 1))
    spread = jnp.where(here, jnp.broadcast_to(recv1[...], shape), 0.0).reshape(NR, 128).astype(BF16)
    coeffs = lax.dot_general(pick, spread, DIMS_NT, preferred_element_type=F32).astype(BF16)
    sums = jnp.dot(coeffs, legv[...], preferred_element_type=F32)
    sums = sums + pltpu.roll(sums, 4, 0)
    other = pltpu.roll(sums, 2, 0)
    even = lax.rem(lane, 2) == 0
    upper = lax.rem(comp, 4) >= 2
    sign = jnp.where(upper & ~even, -1.0, 1.0)
    pieces = []
    for k in range(NT // 128):
        cols = slice(k * 128, (k + 1) * 128)
        row = gain[pl.ds(first_gain + k, 1), :]
        value = jnp.where(even ^ upper, sums[:, cols], other[:, cols]) * (row * sign)
        hi = value.astype(BF16).astype(F32)
        pieces.append(jnp.where(comp < 4, hi, value - hi).astype(BF16))
    filtered = jnp.concatenate(pieces, axis=1)
    cycle = jnp.dot(filtered, leg_turned[...], preferred_element_type=F32)
    cycle = cycle + pltpu.roll(cycle, 4, 0)
    cycle = jnp.dot(cycle.astype(BF16), select[...], preferred_element_type=F32)
    stack = jnp.concatenate([cycle[:, k * 128 : (k + 1) * 128] for k in range(4)], axis=0)
    stack = jnp.transpose(jnp.concatenate([stack, jnp.zeros((96, 128), F32)], axis=0))
    rows = stack[:N_BLK] + pltpu.roll(stack[N_BLK:], 32, 1)
    send2[...] = rows.reshape(N_BLK, 1, 128)
    for peer, to in everyone:
        pltpu.make_async_remote_copy(
            src_ref=send2.at[peer],
            dst_ref=recv2.at[band * N_BLK + blk],
            send_sem=s2,
            recv_sem=r2,
            device_id=(peer, to),
            device_id_type=MESH,
        ).start()
    recv2[band * N_BLK + blk] = send2[blk]
    done2 = pltpu.make_async_remote_copy(
        src_ref=recv2.at[pl.ds(0, N_BLK * N_BAND - 1)],
        dst_ref=recv2.at[pl.ds(0, N_BLK * N_BAND - 1)],
        send_sem=s2,
        recv_sem=r2,
        device_id=(blk, band),
        device_id_type=MESH,
    )
    done2.wait_recv()

    norm = 1.0 / math.sqrt(N_BLK * N_BAND)
    for p in range(2):
        got = jnp.transpose(recv2[pl.ds(p * 128, 128)].reshape(128, 128))[:64]
        modes[:, p * 128 : (p + 1) * 128] = got * norm

    def synthesise(r, carry):
        halves = []
        for h in range(2):
            at = lax.rem(r, 2) * 32 + r // 2 * 8 + 2 * h
            re = modes[pl.ds(at, 1), :]
            im = modes[pl.ds(at + 1, 1), :]
            cosines, sines = wcos[r], wsin[r]
            halves.append(jnp.concatenate([cosines * re - sines * im, sines * re + cosines * im], axis=1))
        z = jnp.concatenate(halves, axis=0).astype(BF16)
        value = jnp.dot(z, table[r], preferred_element_type=F32)
        shape = (2 * A_OWN, B)
        slot = (lax.rem(iota(shape, 0), A_OWN) + band * A_OWN) * B + iota(shape, 1)
        out[pl.ds(r, 2 * A_OWN, stride=R), :] = jnp.where(slot < counts[r], value, 0.0)
        return carry

    lax.fori_loop(0, R, synthesise, 0, unroll=True)
    done1.wait_send()
    done2.wait_send()


def per_device(sky_map, cycle_counts, legendre, signal_power, noise_power):
    sky = sky_map.reshape(2, R, A, B).transpose(0, 2, 1, 3).reshape(2 * A * R, B)
    leg = legendre.reshape(NR, NT)
    vmem = pl.BlockSpec(memory_space=pltpu.VMEM)
    anywhere = pl.BlockSpec(memory_space=pltpu.HBM)
    dma = pltpu.SemaphoreType.DMA
    result = pl.pallas_call(
        kernel,
        out_shape=jax.ShapeDtypeStruct((2 * A_OWN * R, B), F32),
        in_specs=[anywhere] * 5,
        out_specs=vmem,
        scratch_shapes=[
            pltpu.SMEM((R,), jnp.int32),
            pltpu.VMEM((2 * A * R, B), F32),
            pltpu.VMEM((NR, NT), BF16),
            pltpu.VMEM((NT, NR), BF16),
            pltpu.VMEM((64, 128), F32),
            pltpu.VMEM((64, 128), F32),
            pltpu.VMEM((128, 128), F32),
            pltpu.VMEM((N_BLK, 1, 128), F32),
            pltpu.VMEM((N_BLK, 1, 128), F32),
            pltpu.VMEM((N_BLK, 1, 128), F32),
            pltpu.VMEM((N_BAND * N_BLK, 1, 128), F32),
            pltpu.VMEM((64, N_BAND * 64), F32),
            pltpu.VMEM((R, N_BAND * 128, B), BF16),
            pltpu.VMEM((R, A_OWN, N_BAND * 64), F32),
            pltpu.VMEM((R, A_OWN, N_BAND * 64), F32),
            pltpu.VMEM((64, 128), F32),
            pltpu.VMEM((NR, NR), BF16),
            *([dma] * 9),
        ],
        compiler_params=pltpu.CompilerParams(collective_id=0, has_side_effects=True, vmem_limit_bytes=67043328),
    )(cycle_counts, sky, leg, signal_power.reshape(64, 128), noise_power.reshape(64, 128))
    return result.reshape(2, A_OWN, R, B).transpose(0, 2, 1, 3).reshape(2, R, A_OWN * B)


def solution(mesh):
    placed = (P(None, "blk", None), P("blk"), P(None, ("blk", "band"), None), P(), P())
    return jax.shard_map(
        per_device, mesh=mesh, in_specs=placed, out_specs=P(None, "blk", "band"), check_vma=False
    )
```

```python
import math

import jax
import jax.numpy as jnp
from jax import lax
from jax.experimental import pallas as pl
from jax.experimental.pallas import tpu as pltpu
from jax.sharding import PartitionSpec as P

M_FIRST = 2048
N_BLK = 64
N_BAND = 4
R = 8
B = 128
A = 128
A_OWN = A // N_BAND
NR = N_BLK * R
NT = 4096
F32, BF16 = jnp.float32, jnp.bfloat16
MESH = pl.DeviceIdType.MESH
ROUND = 12582912.0
COEFS = (4.442882834158576, -7.308241154915532, 3.606288962930247, -0.8457636193361991, 0.10920579263730913)
DIMS_NT = (((1,), (1,)), ((), ()))


def cos_turns(x, period, inverse):
    whole = (x * inverse + ROUND) - ROUND
    t = (x - whole * period) * inverse
    u = t * t
    p = jnp.full_like(u, COEFS[-1])
    for c in COEFS[-2::-1]:
        p = p * u + c
    s = p * t
    return 1.0 - s * s


def iota(shape, dim):
    return lax.broadcasted_iota(jnp.int32, shape, dim)


def split(x):
    hi = x.astype(BF16)
    return hi, (x - hi.astype(F32)).astype(BF16)


def pixel_table(freq, count, inv_count):
    shape = (B // 8, 8, 128)
    odd = (2 * (iota(shape, 0) * 8 + iota(shape, 1)) + 1).astype(F32)
    quarter = jnp.where(iota((8, 128), 1) >= 64, 0.5 * count, 0.0)
    return cos_turns(odd * freq - quarter, 2.0 * count, 0.5 * inv_count)


def order_table(c, sines, count, inv_count):
    shape = (8, 8, 128)
    row = iota(shape, 0) * 8 + iota(shape, 1)
    freq = (row * N_BAND + (M_FIRST + c)).astype(F32)
    odd = (2 * iota((8, 128), 1) + 1).astype(F32)
    x = freq * odd
    return cos_turns(x + 0.5 * count if sines else x, 2.0 * count, 0.5 * inv_count)


def row_parts(first_row, rows, count, inv_count):
    shape = (rows // 8, 8, 128)
    slot = ((iota(shape, 0) * 8 + iota(shape, 1) + first_row) * B).astype(F32)
    near = jnp.where(slot > 0.5 * count, slot - count, slot)
    near = jnp.where(near > 0.5 * count, near - count, near)
    far = near * 1024.0
    far = far - ((far * inv_count + ROUND) - ROUND) * count
    return near, 2.0 * far


def row_table(parts, offset, count, inv_count, quarter):
    near, far = parts
    return cos_turns(near * offset + (far - quarter), count, inv_count)


def kernel(
    counts_in, sky, leg, signal_in, noise_in, out,
    counts, xs, legv, leg_turned, signal, noise, folded, send1, recv1, send2, recv2, modes, table, wcos, wsin, gain, select,
    count_sem, sky_sem, leg_sem, signal_sem, noise_sem, s1, r1, s2, r2,
):
    blk = lax.axis_index("blk")
    band = lax.axis_index("band")
    barrier = pltpu.get_barrier_semaphore()

    ys = [lax.rem(lax.div(blk, 16) + d, 4) * 16 for d in range(4)]
    zs = [lax.rem(lax.rem(lax.div(blk, 2), 8) + d, 8) * 2 for d in range(8)]
    cs = [lax.rem(blk + d, 2) for d in range(2)]
    steps = [(y, z, c) for y in range(4) for z in range(8) for c in range(2)][1:]
    steps.sort(key=lambda s: -min(s[0], 4 - s[0]) - min(s[1], 8 - s[1]))
    everyone = [(x, s) for x in range(N_BAND) for s in [(0, 0, 0)] + steps][1:]
    everyone.sort(key=lambda t: -min(t[0], 4 - t[0]) - min(t[1][0], 4 - t[1][0]) - min(t[1][1], 8 - t[1][1]))
    bands = [lax.rem(band + x, N_BAND) for x in range(N_BAND)]
    everyone = [(ys[y] + zs[z] + cs[c], bands[x]) for x, (y, z, c) in everyone]
    peers = [ys[y] + zs[z] + cs[c] for y, z, c in steps]

    for peer in peers:
        pl.semaphore_signal(barrier, inc=1, device_id=(peer, band), device_id_type=MESH)
    for e in range(1, N_BAND):
        pl.semaphore_signal(barrier, inc=1, device_id=(blk, lax.rem(band + e, N_BAND)), device_id_type=MESH)
    count_copy = pltpu.make_async_copy(counts_in, counts, count_sem)
    count_copy.start()
    sky_copy = pltpu.make_async_copy(sky, xs, sky_sem)
    sky_copy.start()
    leg_copy = pltpu.make_async_copy(leg, legv, leg_sem)
    leg_copy.start()
    signal_copy = pltpu.make_async_copy(signal_in, signal, signal_sem)
    signal_copy.start()
    noise_copy = pltpu.make_async_copy(noise_in, noise, noise_sem)
    noise_copy.start()

    lane = iota((8, 128), 1)
    own_offset = (lax.rem(lane, 64) * N_BAND + band).astype(F32)
    folded[...] = jnp.zeros_like(folded)
    count_copy.wait()
    sky_copy.wait()

    def count_of(r):
        count = jnp.full((8, 128), counts[r], jnp.int32).astype(F32)
        return count, 1.0 / count

    def analyse(r, carry):
        count, inv_count = count_of(r)
        table = pixel_table(own_offset + M_FIRST, count, inv_count).reshape(B, 128)
        t_hi, t_lo = split(table)
        quarter = jnp.where(lane >= 64, 0.25 * count, 0.0)
        turn = row_table(row_parts(0, A, count, inv_count), own_offset, count, inv_count, quarter)
        swapped = pltpu.roll(turn.reshape(A, 128), 64, 1).reshape(A // 8, 8, 128)
        pixels = xs[pl.ds(r, 2 * A, stride=R), :].reshape(2, A // 8, 8, 128)
        shape = (A // 8, 8, 128)
        slot = ((iota(shape, 0) * 8 + iota(shape, 1)) * B + iota(shape, 2)).astype(F32)
        pixels = jnp.where((slot < count)[None], pixels, 0.0).reshape(2 * A, B)
        x_hi, x_lo = split(pixels)
        part = jnp.dot(
            jnp.concatenate([x_hi, x_lo], axis=1), jnp.concatenate([t_hi, t_hi], axis=0), preferred_element_type=F32
        ) + jnp.dot(x_hi, t_lo, preferred_element_type=F32)
        part = part.reshape(2, A // 8, 8, 128)
        first = jnp.sum(part * turn[None], axis=1)
        second = jnp.sum(part * swapped[None], axis=1)
        first = jnp.concatenate([first[0], first[1]], axis=0)
        second = jnp.concatenate([second[0], second[1]], axis=0)
        scale = lax.rsqrt(count)
        scale = scale * (1.5 - 0.5 * count * scale * scale)
        scale2 = jnp.concatenate([scale, scale], axis=0)
        real = (first - pltpu.roll(first, 64, 1)) * scale2
        imag = -(second + pltpu.roll(second, 64, 1)) * scale2
        parts = (
            real[:8] + real[8:],
            imag[:8] + imag[8:],
            real[:8] - real[8:],
            imag[:8] - imag[8:],
        )
        for k, value in enumerate(parts):
            folded[pl.ds(r * 4 + k, 1), :] = jnp.sum(value, axis=0, keepdims=True)
        return carry

    lax.fori_loop(0, R, analyse, 0)

    turned = jnp.transpose(folded[...])[:N_BLK]
    turned_hi = turned.astype(BF16).astype(F32)
    turned_lo = turned - turned_hi
    lanes64 = iota((N_BLK, 128), 1)
    both = jnp.where(lanes64 < 32, turned_hi, jnp.where(lanes64 < 64, pltpu.roll(turned_lo, 32, 1), 0.0))
    send1[...] = both.reshape(N_BLK, 1, 128)

    pl.semaphore_wait(barrier, N_BLK - 1 + N_BAND - 1)

    def exchange(source, target, send_sem, recv_sem):
        for peer in peers:
            pltpu.make_async_remote_copy(
                src_ref=source.at[peer],
                dst_ref=target.at[blk],
                send_sem=send_sem,
                recv_sem=recv_sem,
                device_id=(peer, band),
                device_id_type=MESH,
            ).start()
        target[blk] = source[blk]
        return pltpu.make_async_remote_copy(
            src_ref=source.at[pl.ds(0, N_BLK - 1)],
            dst_ref=target.at[pl.ds(0, N_BLK - 1)],
            send_sem=send_sem,
            recv_sem=recv_sem,
            device_id=(blk, band),
            device_id_type=MESH,
        )

    done1 = exchange(send1, recv1, s1, r1)

    def prepare(r, carry):
        count, inv_count = count_of(r)
        parts = row_parts(band * A_OWN, A_OWN, count, inv_count)
        for c in range(N_BAND):
            table[r, pl.ds(c * 64, 64), :] = order_table(c, False, count, inv_count).reshape(64, B).astype(BF16)
            table[r, pl.ds(256 + c * 64, 64), :] = order_table(c, True, count, inv_count).reshape(64, B).astype(BF16)
        for p in range(2):
            offset = (lax.rem(lane, 64) * N_BAND + lax.div(lane, 64) + 2 * p).astype(F32)
            cols = pl.ds(p * 128, 128)
            wcos[r, :, cols] = row_table(parts, offset, count, inv_count, 0.0).reshape(A_OWN, 128)
            wsin[r, :, cols] = row_table(parts, offset, count, inv_count, 0.25 * count).reshape(A_OWN, 128)
        return carry

    lax.fori_loop(0, R, prepare, 0)

    leg_copy.wait()

    def turn_legendre(k, carry):
        cols = pl.ds(pl.multiple_of(k * 128, 128), 128)
        leg_turned[cols, :] = jnp.transpose(legv[:, cols])
        return carry

    lax.fori_loop(0, NT // 128, turn_legendre, 0, unroll=2)

    order = blk * N_BAND + band
    low = lax.rem(order, 128)
    signal_copy.wait()
    noise_copy.wait()
    power = signal[...]
    rolled = pltpu.roll(power / (power + noise[...]), lax.rem(128 - low, 128), 1)
    gain[...] = rolled
    following = jnp.concatenate([gain[1:, :], gain[:1, :]], axis=0)
    gain[...] = jnp.where(lanes64 < 128 - low, rolled, following)
    first_gain = M_FIRST // 128 + order // 128

    def permute(k, carry):
        rows = pl.ds(pl.multiple_of(k * 64, 64), 64)
        source = iota((64, NR), 0) + k * 64
        column = iota((64, NR), 1)
        select[rows, :] = jnp.where(lax.rem(column, N_BLK) * R + column // N_BLK == source, 1.0, 0.0).astype(BF16)
        return carry

    lax.fori_loop(0, NR // 64, permute, 0)
    comp = iota((8, 128), 0)
    lane_comp = jnp.where(comp < 4, lane, lane - 32)
    pick = jnp.where(
        (lane_comp >= 0) & (lane_comp < 32) & (lax.rem(lane_comp + 32, 4) == lax.rem(comp, 4)), 1.0, 0.0
    ).astype(BF16)

    done1.wait_recv()

    shape = (N_BLK, 8, 128)
    here = (iota(shape, 2) < 64) & (lax.rem(iota(shape, 2), 32) // 4 == iota(shape, 1))
    spread = jnp.where(here, jnp.broadcast_to(recv1[...], shape), 0.0).reshape(NR, 128).astype(BF16)
    coeffs = lax.dot_general(pick, spread, DIMS_NT, preferred_element_type=F32).astype(BF16)
    sums = jnp.dot(coeffs, legv[...], preferred_element_type=F32)
    sums = sums + pltpu.roll(sums, 4, 0)
    other = pltpu.roll(sums, 2, 0)
    even = lax.rem(lane, 2) == 0
    upper = lax.rem(comp, 4) >= 2
    sign = jnp.where(upper & ~even, -1.0, 1.0)
    pieces = []
    for k in range(NT // 128):
        cols = slice(k * 128, (k + 1) * 128)
        row = gain[pl.ds(first_gain + k, 1), :]
        value = jnp.where(even ^ upper, sums[:, cols], other[:, cols]) * (row * sign)
        hi = value.astype(BF16).astype(F32)
        pieces.append(jnp.where(comp < 4, hi, value - hi).astype(BF16))
    filtered = jnp.concatenate(pieces, axis=1)
    cycle = jnp.dot(filtered, leg_turned[...], preferred_element_type=F32)
    cycle = cycle + pltpu.roll(cycle, 4, 0)
    cycle = jnp.dot(cycle.astype(BF16), select[...], preferred_element_type=F32)
    stack = jnp.concatenate([cycle[:, k * 128 : (k + 1) * 128] for k in range(4)], axis=0)
    stack = jnp.transpose(jnp.concatenate([stack, jnp.zeros((96, 128), F32)], axis=0))
    rows = stack[:N_BLK] + pltpu.roll(stack[N_BLK:], 32, 1)
    send2[...] = rows.reshape(N_BLK, 1, 128)
    for peer, to in everyone:
        pltpu.make_async_remote_copy(
            src_ref=send2.at[peer],
            dst_ref=recv2.at[band * N_BLK + blk],
            send_sem=s2,
            recv_sem=r2,
            device_id=(peer, to),
            device_id_type=MESH,
        ).start()
    recv2[band * N_BLK + blk] = send2[blk]
    done2 = pltpu.make_async_remote_copy(
        src_ref=recv2.at[pl.ds(0, N_BLK * N_BAND - 1)],
        dst_ref=recv2.at[pl.ds(0, N_BLK * N_BAND - 1)],
        send_sem=s2,
        recv_sem=r2,
        device_id=(blk, band),
        device_id_type=MESH,
    )
    done2.wait_recv()

    norm = 1.0 / math.sqrt(N_BLK * N_BAND)
    for p in range(2):
        got = jnp.transpose(recv2[pl.ds(p * 128, 128)].reshape(128, 128))[:64]
        modes[:, p * 128 : (p + 1) * 128] = got * norm

    def synthesise(r, carry):
        halves = []
        for h in range(2):
            at = lax.rem(r, 2) * 32 + r // 2 * 8 + 2 * h
            re = modes[pl.ds(at, 1), :]
            im = modes[pl.ds(at + 1, 1), :]
            cosines, sines = wcos[r], wsin[r]
            halves.append(jnp.concatenate([cosines * re - sines * im, sines * re + cosines * im], axis=1))
        z = jnp.concatenate(halves, axis=0).astype(BF16)
        value = jnp.dot(z, table[r], preferred_element_type=F32)
        shape = (2 * A_OWN, B)
        slot = (lax.rem(iota(shape, 0), A_OWN) + band * A_OWN) * B + iota(shape, 1)
        out[pl.ds(r, 2 * A_OWN, stride=R), :] = jnp.where(slot < counts[r], value, 0.0)
        return carry

    lax.fori_loop(0, R, synthesise, 0, unroll=True)
    done1.wait_send()
    done2.wait_send()


def per_device(sky_map, cycle_counts, legendre, signal_power, noise_power):
    sky = sky_map.reshape(2, R, A, B).transpose(0, 2, 1, 3).reshape(2 * A * R, B)
    leg = legendre.reshape(NR, NT)
    vmem = pl.BlockSpec(memory_space=pltpu.VMEM)
    anywhere = pl.BlockSpec(memory_space=pltpu.HBM)
    dma = pltpu.SemaphoreType.DMA
    result = pl.pallas_call(
        kernel,
        out_shape=jax.ShapeDtypeStruct((2 * A_OWN * R, B), F32),
        in_specs=[anywhere] * 5,
        out_specs=vmem,
        scratch_shapes=[
            pltpu.SMEM((R,), jnp.int32),
            pltpu.VMEM((2 * A * R, B), F32),
            pltpu.VMEM((NR, NT), BF16),
            pltpu.VMEM((NT, NR), BF16),
            pltpu.VMEM((64, 128), F32),
            pltpu.VMEM((64, 128), F32),
            pltpu.VMEM((128, 128), F32),
            pltpu.VMEM((N_BLK, 1, 128), F32),
            pltpu.VMEM((N_BLK, 1, 128), F32),
            pltpu.VMEM((N_BLK, 1, 128), F32),
            pltpu.VMEM((N_BAND * N_BLK, 1, 128), F32),
            pltpu.VMEM((64, N_BAND * 64), F32),
            pltpu.VMEM((R, N_BAND * 128, B), BF16),
            pltpu.VMEM((R, A_OWN, N_BAND * 64), F32),
            pltpu.VMEM((R, A_OWN, N_BAND * 64), F32),
            pltpu.VMEM((64, 128), F32),
            pltpu.VMEM((NR, NR), BF16),
            *([dma] * 9),
        ],
        compiler_params=pltpu.CompilerParams(collective_id=0, has_side_effects=True, vmem_limit_bytes=32 << 20),
    )(*[pltpu.with_memory_space_constraint(x, pltpu.HBM) for x in (cycle_counts, sky, leg, signal_power.reshape(64, 128), noise_power.reshape(64, 128))])
    return result.reshape(2, A_OWN, R, B).transpose(0, 2, 1, 3).reshape(2, R, A_OWN * B)


def solution(mesh):
    placed = (P(None, "blk", None), P("blk"), P(None, ("blk", "band"), None), P(), P())
    return jax.shard_map(
        per_device, mesh=mesh, in_specs=placed, out_specs=P(None, "blk", "band"), check_vma=False
    )
```

```python
import math

import jax
import jax.numpy as jnp
from jax import lax
from jax.experimental import pallas as pl
from jax.experimental.pallas import tpu as pltpu
from jax.sharding import PartitionSpec as P

M_FIRST = 2048
N_BLK = 64
N_BAND = 4
R = 8
B = 128
A = 128
A_OWN = A // N_BAND
NR = N_BLK * R
NT = 4096
F32, BF16 = jnp.float32, jnp.bfloat16
MESH = pl.DeviceIdType.MESH
ROUND = 12582912.0
COEFS = (4.442882834158576, -7.308241154915532, 3.606288962930247, -0.8457636193361991, 0.10920579263730913)
DIMS_NT = (((1,), (1,)), ((), ()))


def cos_turns(x, period, inverse):
    whole = (x * inverse + ROUND) - ROUND
    t = (x - whole * period) * inverse
    u = t * t
    p = jnp.full_like(u, COEFS[-1])
    for c in COEFS[-2::-1]:
        p = p * u + c
    s = p * t
    return 1.0 - s * s


def iota(shape, dim):
    return lax.broadcasted_iota(jnp.int32, shape, dim)


def split(x):
    hi = x.astype(BF16)
    return hi, (x - hi.astype(F32)).astype(BF16)


def pixel_table(freq, count, inv_count):
    shape = (B // 8, 8, 128)
    odd = (2 * (iota(shape, 0) * 8 + iota(shape, 1)) + 1).astype(F32)
    quarter = jnp.where(iota((8, 128), 1) >= 64, 0.5 * count, 0.0)
    return cos_turns(odd * freq - quarter, 2.0 * count, 0.5 * inv_count)


def order_table(c, sines, count, inv_count):
    shape = (8, 8, 128)
    row = iota(shape, 0) * 8 + iota(shape, 1)
    freq = (row * N_BAND + (M_FIRST + c)).astype(F32)
    odd = (2 * iota((8, 128), 1) + 1).astype(F32)
    x = freq * odd
    return cos_turns(x + 0.5 * count if sines else x, 2.0 * count, 0.5 * inv_count)


def row_parts(first_row, rows, count, inv_count):
    shape = (rows // 8, 8, 128)
    slot = ((iota(shape, 0) * 8 + iota(shape, 1) + first_row) * B).astype(F32)
    near = jnp.where(slot > 0.5 * count, slot - count, slot)
    near = jnp.where(near > 0.5 * count, near - count, near)
    far = near * 1024.0
    far = far - ((far * inv_count + ROUND) - ROUND) * count
    return near, 2.0 * far


def row_table(parts, offset, count, inv_count, quarter):
    near, far = parts
    return cos_turns(near * offset + (far - quarter), count, inv_count)


def kernel(
    counts_in, sky, leg, signal_in, noise_in, out,
    counts, xs, legv, leg_turned, signal, noise, folded, send1, recv1, send2, recv2, modes, table, wcos, wsin, gain, select,
    count_sem, sky_sem, leg_sem, signal_sem, noise_sem, s1, r1, s2, r2,
):
    blk = lax.axis_index("blk")
    band = lax.axis_index("band")
    count_copy = pltpu.make_async_copy(counts_in, counts, count_sem)
    count_copy.start()
    sky_copy = pltpu.make_async_copy(sky, xs, sky_sem)
    sky_copy.start()
    barrier = pltpu.get_barrier_semaphore()

    ys = [lax.rem(lax.div(blk, 16) + d, 4) * 16 for d in range(4)]
    zs = [lax.rem(lax.rem(lax.div(blk, 2), 8) + d, 8) * 2 for d in range(8)]
    cs = [lax.rem(blk + d, 2) for d in range(2)]
    steps = [(y, z, c) for y in range(4) for z in range(8) for c in range(2)][1:]
    steps.sort(key=lambda s: -min(s[0], 4 - s[0]) - min(s[1], 8 - s[1]))
    everyone = [(x, s) for x in range(N_BAND) for s in [(0, 0, 0)] + steps][1:]
    everyone.sort(key=lambda t: -min(t[0], 4 - t[0]) - min(t[1][0], 4 - t[1][0]) - min(t[1][1], 8 - t[1][1]))
    bands = [lax.rem(band + x, N_BAND) for x in range(N_BAND)]
    everyone = [(ys[y] + zs[z] + cs[c], bands[x]) for x, (y, z, c) in everyone]
    peers = [ys[y] + zs[z] + cs[c] for y, z, c in steps]

    for peer in peers:
        pl.semaphore_signal(barrier, inc=1, device_id=(peer, band), device_id_type=MESH)
    for e in range(1, N_BAND):
        pl.semaphore_signal(barrier, inc=1, device_id=(blk, lax.rem(band + e, N_BAND)), device_id_type=MESH)
    leg_copy = pltpu.make_async_copy(leg, legv, leg_sem)
    leg_copy.start()
    signal_copy = pltpu.make_async_copy(signal_in, signal, signal_sem)
    signal_copy.start()
    noise_copy = pltpu.make_async_copy(noise_in, noise, noise_sem)
    noise_copy.start()

    lane = iota((8, 128), 1)
    own_offset = (lax.rem(lane, 64) * N_BAND + band).astype(F32)
    folded[...] = jnp.zeros_like(folded)
    count_copy.wait()
    sky_copy.wait()

    def count_of(r):
        count = jnp.full((8, 128), counts[r], jnp.int32).astype(F32)
        return count, 1.0 / count

    def analyse(r, carry):
        count, inv_count = count_of(r)
        table = pixel_table(own_offset + M_FIRST, count, inv_count).reshape(B, 128)
        t_hi, t_lo = split(table)
        quarter = jnp.where(lane >= 64, 0.25 * count, 0.0)
        turn = row_table(row_parts(0, A, count, inv_count), own_offset, count, inv_count, quarter)
        swapped = pltpu.roll(turn.reshape(A, 128), 64, 1).reshape(A // 8, 8, 128)
        pixels = xs[pl.ds(r, 2 * A, stride=R), :].reshape(2, A // 8, 8, 128)
        shape = (A // 8, 8, 128)
        slot = ((iota(shape, 0) * 8 + iota(shape, 1)) * B + iota(shape, 2)).astype(F32)
        pixels = jnp.where((slot < count)[None], pixels, 0.0).reshape(2 * A, B)
        x_hi, x_lo = split(pixels)
        part = jnp.dot(
            jnp.concatenate([x_hi, x_lo], axis=1), jnp.concatenate([t_hi, t_hi], axis=0), preferred_element_type=F32
        ) + jnp.dot(x_hi, t_lo, preferred_element_type=F32)
        part = part.reshape(2, A // 8, 8, 128)
        first = jnp.sum(part * turn[None], axis=1)
        second = jnp.sum(part * swapped[None], axis=1)
        first = jnp.concatenate([first[0], first[1]], axis=0)
        second = jnp.concatenate([second[0], second[1]], axis=0)
        scale = lax.rsqrt(count)
        scale = scale * (1.5 - 0.5 * count * scale * scale)
        scale2 = jnp.concatenate([scale, scale], axis=0)
        real = (first - pltpu.roll(first, 64, 1)) * scale2
        imag = -(second + pltpu.roll(second, 64, 1)) * scale2
        parts = (
            real[:8] + real[8:],
            imag[:8] + imag[8:],
            real[:8] - real[8:],
            imag[:8] - imag[8:],
        )
        for k, value in enumerate(parts):
            folded[pl.ds(r * 4 + k, 1), :] = jnp.sum(value, axis=0, keepdims=True)
        return carry

    lax.fori_loop(0, R, analyse, 0)

    turned = jnp.transpose(folded[...])[:N_BLK]
    turned_hi = turned.astype(BF16).astype(F32)
    turned_lo = turned - turned_hi
    lanes64 = iota((N_BLK, 128), 1)
    both = jnp.where(lanes64 < 32, turned_hi, jnp.where(lanes64 < 64, pltpu.roll(turned_lo, 32, 1), 0.0))
    send1[...] = both.reshape(N_BLK, 1, 128)

    pl.semaphore_wait(barrier, N_BLK - 1 + N_BAND - 1)

    def exchange(source, target, send_sem, recv_sem):
        for peer in peers:
            pltpu.make_async_remote_copy(
                src_ref=source.at[peer],
                dst_ref=target.at[blk],
                send_sem=send_sem,
                recv_sem=recv_sem,
                device_id=(peer, band),
                device_id_type=MESH,
            ).start()
        target[blk] = source[blk]
        return pltpu.make_async_remote_copy(
            src_ref=source.at[pl.ds(0, N_BLK - 1)],
            dst_ref=target.at[pl.ds(0, N_BLK - 1)],
            send_sem=send_sem,
            recv_sem=recv_sem,
            device_id=(blk, band),
            device_id_type=MESH,
        )

    done1 = exchange(send1, recv1, s1, r1)

    def prepare(r, carry):
        count, inv_count = count_of(r)
        parts = row_parts(band * A_OWN, A_OWN, count, inv_count)
        for c in range(N_BAND):
            table[r, pl.ds(c * 64, 64), :] = order_table(c, False, count, inv_count).reshape(64, B).astype(BF16)
            table[r, pl.ds(256 + c * 64, 64), :] = order_table(c, True, count, inv_count).reshape(64, B).astype(BF16)
        for p in range(2):
            offset = (lax.rem(lane, 64) * N_BAND + lax.div(lane, 64) + 2 * p).astype(F32)
            cols = pl.ds(p * 128, 128)
            wcos[r, :, cols] = row_table(parts, offset, count, inv_count, 0.0).reshape(A_OWN, 128)
            wsin[r, :, cols] = row_table(parts, offset, count, inv_count, 0.25 * count).reshape(A_OWN, 128)
        return carry

    lax.fori_loop(0, R, prepare, 0)

    leg_copy.wait()

    def turn_legendre(k, carry):
        cols = pl.ds(pl.multiple_of(k * 128, 128), 128)
        leg_turned[cols, :] = jnp.transpose(legv[:, cols])
        return carry

    lax.fori_loop(0, NT // 128, turn_legendre, 0, unroll=2)

    order = blk * N_BAND + band
    low = lax.rem(order, 128)
    signal_copy.wait()
    noise_copy.wait()
    power = signal[...]
    rolled = pltpu.roll(power / (power + noise[...]), lax.rem(128 - low, 128), 1)
    gain[...] = rolled
    following = jnp.concatenate([gain[1:, :], gain[:1, :]], axis=0)
    gain[...] = jnp.where(lanes64 < 128 - low, rolled, following)
    first_gain = M_FIRST // 128 + order // 128

    def permute(k, carry):
        rows = pl.ds(pl.multiple_of(k * 64, 64), 64)
        source = iota((64, NR), 0) + k * 64
        column = iota((64, NR), 1)
        select[rows, :] = jnp.where(lax.rem(column, N_BLK) * R + column // N_BLK == source, 1.0, 0.0).astype(BF16)
        return carry

    lax.fori_loop(0, NR // 64, permute, 0)
    comp = iota((8, 128), 0)
    lane_comp = jnp.where(comp < 4, lane, lane - 32)
    pick = jnp.where(
        (lane_comp >= 0) & (lane_comp < 32) & (lax.rem(lane_comp + 32, 4) == lax.rem(comp, 4)), 1.0, 0.0
    ).astype(BF16)

    done1.wait_recv()

    shape = (N_BLK, 8, 128)
    here = (iota(shape, 2) < 64) & (lax.rem(iota(shape, 2), 32) // 4 == iota(shape, 1))
    spread = jnp.where(here, jnp.broadcast_to(recv1[...], shape), 0.0).reshape(NR, 128).astype(BF16)
    coeffs = lax.dot_general(pick, spread, DIMS_NT, preferred_element_type=F32).astype(BF16)
    sums = jnp.dot(coeffs, legv[...], preferred_element_type=F32)
    sums = sums + pltpu.roll(sums, 4, 0)
    other = pltpu.roll(sums, 2, 0)
    even = lax.rem(lane, 2) == 0
    upper = lax.rem(comp, 4) >= 2
    sign = jnp.where(upper & ~even, -1.0, 1.0)
    pieces = []
    for k in range(NT // 128):
        cols = slice(k * 128, (k + 1) * 128)
        row = gain[pl.ds(first_gain + k, 1), :]
        value = jnp.where(even ^ upper, sums[:, cols], other[:, cols]) * (row * sign)
        hi = value.astype(BF16).astype(F32)
        pieces.append(jnp.where(comp < 4, hi, value - hi).astype(BF16))
    filtered = jnp.concatenate(pieces, axis=1)
    cycle = jnp.dot(filtered, leg_turned[...], preferred_element_type=F32)
    cycle = cycle + pltpu.roll(cycle, 4, 0)
    cycle = jnp.dot(cycle.astype(BF16), select[...], preferred_element_type=F32)
    stack = jnp.concatenate([cycle[:, k * 128 : (k + 1) * 128] for k in range(4)], axis=0)
    stack = jnp.transpose(jnp.concatenate([stack, jnp.zeros((96, 128), F32)], axis=0))
    rows = stack[:N_BLK] + pltpu.roll(stack[N_BLK:], 32, 1)
    send2[...] = rows.reshape(N_BLK, 1, 128)
    for peer, to in everyone:
        pltpu.make_async_remote_copy(
            src_ref=send2.at[peer],
            dst_ref=recv2.at[band * N_BLK + blk],
            send_sem=s2,
            recv_sem=r2,
            device_id=(peer, to),
            device_id_type=MESH,
        ).start()
    recv2[band * N_BLK + blk] = send2[blk]
    done2 = pltpu.make_async_remote_copy(
        src_ref=recv2.at[pl.ds(0, N_BLK * N_BAND - 1)],
        dst_ref=recv2.at[pl.ds(0, N_BLK * N_BAND - 1)],
        send_sem=s2,
        recv_sem=r2,
        device_id=(blk, band),
        device_id_type=MESH,
    )
    done2.wait_recv()

    norm = 1.0 / math.sqrt(N_BLK * N_BAND)
    for p in range(2):
        got = jnp.transpose(recv2[pl.ds(p * 128, 128)].reshape(128, 128))[:64]
        modes[:, p * 128 : (p + 1) * 128] = got * norm

    def synthesise(r, carry):
        halves = []
        for h in range(2):
            at = lax.rem(r, 2) * 32 + r // 2 * 8 + 2 * h
            re = modes[pl.ds(at, 1), :]
            im = modes[pl.ds(at + 1, 1), :]
            cosines, sines = wcos[r], wsin[r]
            halves.append(jnp.concatenate([cosines * re - sines * im, sines * re + cosines * im], axis=1))
        z = jnp.concatenate(halves, axis=0).astype(BF16)
        value = jnp.dot(z, table[r], preferred_element_type=F32)
        shape = (2 * A_OWN, B)
        slot = (lax.rem(iota(shape, 0), A_OWN) + band * A_OWN) * B + iota(shape, 1)
        out[pl.ds(r, 2 * A_OWN, stride=R), :] = jnp.where(slot < counts[r], value, 0.0)
        return carry

    lax.fori_loop(0, R, synthesise, 0, unroll=True)
    done1.wait_send()
    done2.wait_send()


def per_device(sky_map, cycle_counts, legendre, signal_power, noise_power):
    sky = sky_map.reshape(2, R, A, B).transpose(0, 2, 1, 3).reshape(2 * A * R, B)
    leg = legendre.reshape(NR, NT)
    vmem = pl.BlockSpec(memory_space=pltpu.VMEM)
    anywhere = pl.BlockSpec(memory_space=pltpu.HBM)
    dma = pltpu.SemaphoreType.DMA
    result = pl.pallas_call(
        kernel,
        out_shape=jax.ShapeDtypeStruct((2 * A_OWN * R, B), F32),
        in_specs=[anywhere] * 5,
        out_specs=vmem,
        scratch_shapes=[
            pltpu.SMEM((R,), jnp.int32),
            pltpu.VMEM((2 * A * R, B), F32),
            pltpu.VMEM((NR, NT), BF16),
            pltpu.VMEM((NT, NR), BF16),
            pltpu.VMEM((64, 128), F32),
            pltpu.VMEM((64, 128), F32),
            pltpu.VMEM((128, 128), F32),
            pltpu.VMEM((N_BLK, 1, 128), F32),
            pltpu.VMEM((N_BLK, 1, 128), F32),
            pltpu.VMEM((N_BLK, 1, 128), F32),
            pltpu.VMEM((N_BAND * N_BLK, 1, 128), F32),
            pltpu.VMEM((64, N_BAND * 64), F32),
            pltpu.VMEM((R, N_BAND * 128, B), BF16),
            pltpu.VMEM((R, A_OWN, N_BAND * 64), F32),
            pltpu.VMEM((R, A_OWN, N_BAND * 64), F32),
            pltpu.VMEM((64, 128), F32),
            pltpu.VMEM((NR, NR), BF16),
            *([dma] * 9),
        ],
        compiler_params=pltpu.CompilerParams(collective_id=0, has_side_effects=True, vmem_limit_bytes=32 << 20),
    )(*[pltpu.with_memory_space_constraint(x, pltpu.HBM) for x in (cycle_counts, sky, leg, signal_power.reshape(64, 128), noise_power.reshape(64, 128))])
    return result.reshape(2, A_OWN, R, B).transpose(0, 2, 1, 3).reshape(2, R, A_OWN * B)


def solution(mesh):
    placed = (P(None, "blk", None), P("blk"), P(None, ("blk", "band"), None), P(), P())
    return jax.shard_map(
        per_device, mesh=mesh, in_specs=placed, out_specs=P(None, "blk", "band"), check_vma=False
    )
```
